128 devices in a mesh: req: 64 (over z, y, x), ctx: 2 (over core).
Axes of the slice: x: 4, y: 4, z: 4, core: 2. Of those that a mesh axis runs over, the one named last changes fastest.
Arguments:
- conv_input: bfloat16 [64, 512, 10240], P('req', 'ctx'), may hold values from -6 to 6
- gate_input: bfloat16 [64, 512, 8192], P('req', 'ctx'), may hold values from -6 to 6
- dt_raw: bfloat16 [64, 512, 128], P('req', 'ctx'), may hold values from -3 to 3
- conv_weight: float32 [4, 10240], replicated, may hold values from -3 to 3
- conv_bias: float32 [10240], replicated, may hold values from -3 to 3
- dt_bias: float32 [128], replicated
- a_log: float32 [128], replicated
- d_skip: float32 [128], replicated, may hold values from 0.5 to 2
- norm_weight: float32 [8192], replicated, may hold values from 0.5 to 1.5
- conv_cache: bfloat16 [64, 3, 10240], P('req'), may hold values from -6 to 6
- state_pool: float32 [16384, 64, 128], P(('req', 'ctx')), may hold values from -6 to 6
- page_owner: int32 [64, 128], replicated, may hold values from 0 to 127, as said below
- page_slot: int32 [64, 128], replicated, may hold values from 0 to 127, as said below
- prefix_len: int32 [64], replicated, may hold values from 0 to 32767, as said below
- new_count: int32 [64], replicated, may hold values from 64 to 512, as said below
Outputs:
- mixed: bfloat16 [64, 512, 8192], P('req', 'ctx')
- new_conv: bfloat16 [64, 3, 10240], P('req')
- new_pool: float32 [16384, 64, 128], P(('req', 'ctx'))
The draws below stay inside these ranges and needn't reach their ends.
Inputs may be any that keep to these rules, and one draw needn't show every extreme that they name: `page_owner`: page j of request r holds rows j * 64 to (j + 1) * 64 - 1 of its state; devices are counted as req index times the ctx axis's size plus ctx index. The 64 pages j of one request with the same j // 64 lie on different devices, and every device holds exactly 64 pages of all requests together. `page_slot`: the pages held by one device lie in different slots; other slots hold nothing of these requests. `prefix_len`: some request has prefix length 0 in every draw. `new_count`: both ends are reached in every draw; the new tokens of a request fill its first slots.
All inputs are finite; a program needn't handle non-finite values.
Results may differ from the reference program's by a relative error of at most 0.0095.
Values may be sent and summed in bfloat16 or wider, within the bound.
No kernel may reach another device: no remote copies, remote signals or barrier semaphores. Data moves between devices by JAX's collectives and lax.ppermute only.
A program may use at most 192 MiB of HBM per device.

```python
import math
import jax
import jax.numpy as jnp
from jax import lax

HEADS = 128
HDIM = 64
NSTATE = 128
GROUPS = 8
KCONV = 4
TOK_DEV = 256
INNER = 8192
CONVDIM = 10240
LEN = 512
REQS = 64
PPD = 64
PAGES = 128
PAGE_ROWS = 64
POOL_DEV = 128
SLOTS = 16384
N_REQ = 64
N_CTX = 2


def page_tables(key):
    base = jax.random.fold_in(key, 11)
    keys = jax.random.split(base, 4)
    devices = N_REQ * N_CTX
    sigma = jax.random.permutation(keys[0], devices)
    tau = jax.random.permutation(keys[1], devices)
    offsets = jax.random.permutation(keys[2], devices)[:PPD]
    position = (tau[:, None] + offsets[None, :]) % devices
    owner = sigma[position]
    slot_keys = jax.random.split(keys[3], devices)
    orders = jax.vmap(lambda single: jax.random.permutation(single, POOL_DEV))(slot_keys)
    slot = orders[owner, jnp.arange(PPD, dtype=jnp.int32)[None, :]]
    return (owner.reshape(N_REQ, PAGES).astype(jnp.int32), slot.reshape(N_REQ, PAGES).astype(jnp.int32))


def draw_page_owner(key, part):
    return page_tables(key)[0]


def draw_page_slot(key, part):
    return page_tables(key)[1]


def head_rates(key):
    base = jax.random.fold_in(key, 41)
    keys = jax.random.split(base, 4)
    target = jnp.exp(jax.random.uniform(keys[0], (HEADS,), jnp.float32, math.log(0.01), math.log(0.1)))
    share = 0.5
    slow = jax.random.uniform(keys[1], (HEADS,), jnp.float32) < share
    slow_rate = jnp.exp(jax.random.uniform(keys[2], (HEADS,), jnp.float32, jnp.log(0.3 / LEN), jnp.log(1.5 / LEN)))
    fast_rate = jnp.exp(jax.random.uniform(keys[3], (HEADS,), jnp.float32, math.log(1.0 / 50.0), math.log(1.0 / 30.0)))
    return (target, jnp.where(slow, slow_rate, fast_rate))


def draw_dt_bias(key, part):
    target, rate = head_rates(key)
    return jnp.log(jnp.expm1(target)).astype(jnp.float32)


def draw_a_log(key, part):
    target, rate = head_rates(key)
    return jnp.log(rate / target).astype(jnp.float32)


def draw_prefix_len(key, part):
    keys = jax.random.split(jax.random.fold_in(key, 23), 4)
    coin = jax.random.randint(keys[0], (REQS,), 0, 4) == 0
    small = jax.random.randint(keys[1], (REQS,), 0, 3)
    large = jax.random.randint(keys[2], (REQS,), 3, 32768)
    values = jnp.where(coin, small, large)
    order = jax.random.permutation(keys[3], REQS)
    values = values.at[order[0]].set(0).at[order[1]].set(32767)
    return values.astype(jnp.int32)


def draw_new_count(key, part):
    keys = jax.random.split(jax.random.fold_in(key, 29), 2)
    lowest = max(LEN // 8, KCONV)
    values = jax.random.randint(keys[0], (REQS,), lowest, LEN + 1)
    order = jax.random.permutation(keys[1], REQS)
    values = values.at[order[0]].set(LEN).at[order[1]].set(lowest)
    return values.astype(jnp.int32)


def block_scale(own_key, extent, cuts, smallest, top_value):
    loudness = 1.0
    for dim, blocks in cuts:
        heights = jax.random.uniform(jax.random.fold_in(jax.random.fold_in(own_key, 6), dim), (blocks,), jnp.float32, smallest / len(cuts), top_value / len(cuts))
        loudness = loudness * jnp.repeat(jnp.exp(heights), extent[dim] // blocks).reshape((-1,) + (1,) * (len(extent) - 1 - dim))
    return loudness


def centred(key, shape, scale, limit, pieces=(), held_as=jnp.bfloat16):
    drawn = jax.random.normal(key, shape, jnp.float32) * scale
    if len(pieces) > 0:
        drawn = block_scale(key, shape, pieces, -0.22, 0.18) * drawn
    return jnp.clip(drawn, min=-limit, max=limit).astype(held_as)


def setup_inputs(seed: int = 0) -> dict:
    arg_keys = jax.random.split(jax.random.key(seed), 16)
    return {
        "conv_input": centred(arg_keys[0], (REQS, LEN, CONVDIM), 1.0, 6.0, ((0, 64), (1, 2))),
        "gate_input": centred(arg_keys[1], (REQS, LEN, INNER), 1.0, 6.0, ((0, 64), (1, 2))),
        "dt_raw": centred(arg_keys[2], (REQS, LEN, HEADS), 0.5, 3.0, ((0, 64), (1, 2))),
        "conv_weight": centred(arg_keys[3], (KCONV, CONVDIM), KCONV ** -0.5, 3.0, (), jnp.float32),
        "conv_bias": centred(arg_keys[4], (CONVDIM,), 0.5, 3.0, (), jnp.float32),
        "dt_bias": draw_dt_bias(jax.random.fold_in(arg_keys[15], 71), 0),
        "a_log": draw_a_log(jax.random.fold_in(arg_keys[15], 71), 0),
        "d_skip": jnp.clip(jax.random.uniform(arg_keys[7], (HEADS,), jnp.float32, 0.5, 2.0), 0.5, 2.0),
        "norm_weight": jnp.clip(1.0 + 0.1 * jax.random.normal(arg_keys[8], (INNER,), jnp.float32), 0.5, 1.5),
        "conv_cache": centred(arg_keys[9], (REQS, KCONV - 1, CONVDIM), 1.0, 6.0, ((0, 64),)),
        "state_pool": centred(arg_keys[10], (SLOTS, PAGE_ROWS, NSTATE), 1.0, 6.0, ((0, 128),), jnp.float32),
        "page_owner": draw_page_owner(jax.random.fold_in(arg_keys[15], 71), 0),
        "page_slot": draw_page_slot(jax.random.fold_in(arg_keys[15], 71), 0),
        "prefix_len": draw_prefix_len(jax.random.fold_in(arg_keys[15], 71), 0),
        "new_count": draw_new_count(jax.random.fold_in(arg_keys[15], 71), 0),
    }


def conv_silu(extended, conv_weight, conv_bias, count_rows):
    accum = jnp.broadcast_to(conv_bias, (count_rows, conv_bias.shape[0])).astype(jnp.float32)
    for tap in range(conv_weight.shape[0]):
        accum = accum + conv_weight[tap] * extended[tap:tap + count_rows].astype(jnp.float32)
    return jax.nn.silu(accum).astype(jnp.bfloat16)

def local_block(inputs, b_proj, c_proj, step_size, log_decay):
    rows, heads, width = inputs.shape
    groups = b_proj.shape[1]
    per_group = heads // groups
    cumulative = jnp.cumsum(log_decay, axis=0)
    lower = jnp.arange(rows, dtype=jnp.int32)[:, None] >= jnp.arange(rows, dtype=jnp.int32)[None, :]
    grouped_x = jnp.moveaxis(inputs.reshape(rows, groups, per_group, width), 1, 0)
    grouped_cum = jnp.moveaxis(cumulative.reshape(rows, groups, per_group), 1, 0)
    grouped_dt = jnp.moveaxis(step_size.reshape(rows, groups, per_group), 1, 0)

    def per_head_group(items):
        x_grp, b_grp, c_grp, cum_grp, dt_grp = items
        scores = jnp.dot(c_grp, b_grp.T, preferred_element_type=jnp.float32)
        gap = cum_grp.T[:, :, None] - cum_grp.T[:, None, :]
        decay = jnp.where(lower, jnp.exp(jnp.where(lower, gap, 0.0)), 0.0)
        weights = lax.optimization_barrier((scores[None] * decay * dt_grp.T[:, None, :]).astype(jnp.bfloat16))
        intra = jnp.einsum('hts,shp->thp', weights.astype(jnp.float32), x_grp.astype(jnp.float32), precision=lax.Precision.HIGHEST)
        ending = jnp.exp(cum_grp[-1][None, :] - cum_grp) * dt_grp
        scaled = lax.optimization_barrier((x_grp.astype(jnp.float32) * ending[:, :, None]).astype(jnp.bfloat16))
        state = jnp.einsum('shp,sn->hpn', scaled.astype(jnp.float32), b_grp.astype(jnp.float32), precision=lax.Precision.HIGHEST)
        return (intra, state)
    intra, states = lax.map(per_head_group, (grouped_x, jnp.moveaxis(b_proj, 1, 0), jnp.moveaxis(c_proj, 1, 0), grouped_cum, grouped_dt))
    intra = jnp.moveaxis(intra, 0, 1).reshape(rows, heads, width)
    return (intra, states.reshape(heads, width, -1), cumulative)

def state_part(c_proj, cumulative, state):
    rows, groups, _ = c_proj.shape
    heads = cumulative.shape[1]
    rounded = lax.optimization_barrier(state.astype(jnp.bfloat16)).reshape(groups, -1, state.shape[2])
    product = jnp.einsum('tgn,gkn->tgk', c_proj.astype(jnp.float32), rounded.astype(jnp.float32), precision=lax.Precision.HIGHEST)
    return product.reshape(rows, heads, -1) * jnp.exp(cumulative)[:, :, None]

def finish(mixer, inputs, gate_in, d_skip, norm_weight, live, groups):
    rows = mixer.shape[0]
    summed = mixer + d_skip[None, :, None] * inputs.astype(jnp.float32)
    gated = summed.reshape(rows, -1) * jax.nn.silu(gate_in.astype(jnp.float32))
    grouped = gated.reshape(rows, groups, -1)
    factor = lax.rsqrt(lax.optimization_barrier(jnp.mean(grouped * grouped, axis=-1, keepdims=True)) + 1e-05)
    normed = (grouped * factor).reshape(rows, -1) * norm_weight
    return jnp.where(live[:, None], normed, 0.0).astype(jnp.bfloat16)

def reference(conv_input, gate_input, dt_raw, conv_weight, conv_bias, dt_bias, a_log, d_skip, norm_weight, conv_cache, state_pool, page_owner, page_slot, prefix_len, new_count):
    decay_rate = -jnp.exp(a_log)
    rim = KCONV - 1
    blocks = LEN // TOK_DEV
    global_slot = (page_owner * POOL_DEV + page_slot).astype(jnp.int32)

    def one_request(request):
        tokens = conv_input[request]
        prefix = prefix_len[request]
        count = new_count[request]
        keep_rows = jnp.arange(rim, dtype=jnp.int32) >= rim - prefix
        cached = jnp.where(keep_rows[:, None], conv_cache[request], jnp.zeros_like(conv_cache[request]))
        extended = jnp.concatenate([cached, tokens], axis=0)
        active = conv_silu(extended, conv_weight, conv_bias, LEN)
        inputs = active[:, :INNER].reshape(LEN, HEADS, HDIM)
        b_proj = active[:, INNER:INNER + GROUPS * NSTATE].reshape(LEN, GROUPS, NSTATE)
        c_proj = active[:, INNER + GROUPS * NSTATE:].reshape(LEN, GROUPS, NSTATE)
        live = jnp.arange(LEN, dtype=jnp.int32) < count
        step_size = jax.nn.softplus(dt_raw[request].astype(jnp.float32) + dt_bias) * live[:, None].astype(jnp.float32)
        log_decay = step_size * decay_rate
        initial = state_pool[global_slot[request]].reshape(HEADS, HDIM, NSTATE) * (prefix > 0).astype(jnp.float32)

        def per_block(state, items):
            x_blk, b_blk, c_blk, dt_blk, la_blk, gate_blk, live_blk = items
            intra, local_state, cumulative = local_block(x_blk, b_blk, c_blk, dt_blk, la_blk)
            carried = state_part(c_blk, cumulative, state)
            output = finish(intra + carried, x_blk, gate_blk, d_skip, norm_weight, live_blk, GROUPS)
            following = jnp.exp(cumulative[-1])[:, None, None] * state + local_state
            return (following, output)

        def blocked(array):
            return array.reshape((blocks, TOK_DEV) + array.shape[1:])
        final, outputs = lax.scan(per_block, initial, (blocked(inputs), blocked(b_proj), blocked(c_proj), blocked(step_size), blocked(log_decay), blocked(gate_input[request]), blocked(live)))
        tail = lax.dynamic_slice_in_dim(tokens, (count - rim).astype(jnp.int32), rim, 0)
        return (outputs.reshape(LEN, INNER), tail, final)
    mixed, tails, finals = lax.map(one_request, jnp.arange(REQS, dtype=jnp.int32))
    pages = finals.reshape(REQS * PAGES, PAGE_ROWS, NSTATE)
    new_pool = state_pool.at[global_slot.reshape(-1)].set(pages)
    return (mixed, tails, new_pool)
```

```python
import jax
import jax.numpy as jnp
from jax import lax
from jax.experimental import pallas as pl
from jax.experimental.pallas import tpu as pltpu
from jax.sharding import PartitionSpec as P

GROUPS = 8
LANES = 128
TOP = 88.72
F32 = jnp.float32
BF16 = jnp.bfloat16


def swapped(value):
    return lax.ppermute(value, "ctx", [(0, 1), (1, 0)])


def silu(value):
    half = 0.5 * value
    return half + half * jnp.tanh(half)


def cost(flops, nbytes, trans=0):
    return pl.CostEstimate(flops=flops, bytes_accessed=nbytes, transcendentals=trans)


def gather_body(dev_ref, pool_ref, out_ref):
    step = pl.program_id(0)
    for k in range(pool_ref.shape[0]):
        device = dev_ref[step * pool_ref.shape[0] + k]

        @pl.when(device >= 0)
        def _():
            out_ref[device] = pool_ref[k].astype(BF16)


def gather_pages(dev_of_slot, pool, devices):
    slots, rows, width = pool.shape
    chunk = min(32, slots)
    return pl.pallas_call(
        gather_body,
        out_shape=jax.ShapeDtypeStruct((devices, rows, width), BF16),
        grid_spec=pltpu.PrefetchScalarGridSpec(
            num_scalar_prefetch=1,
            grid=(slots // chunk,),
            in_specs=[pl.BlockSpec((chunk, rows, width), lambda i, d: (i, 0, 0))],
            out_specs=pl.BlockSpec((devices, rows, width), lambda i, d: (0, 0, 0)),
        ),
        cost_estimate=cost(slots * rows * width, slots * rows * width * 6),
        name="gather_pages",
    )(dev_of_slot, pool)


def steps_body(at_ref, raw_ref, bias_ref, alog_ref, cum_ref, shift_ref, ending_ref, decay_ref):
    rows, heads = cum_ref.shape
    pos = at_ref[0] + lax.broadcasted_iota(jnp.int32, (rows, heads), 0)
    live = pos < at_ref[1]
    value = raw_ref[0].astype(F32) + bias_ref[...]
    soft = jnp.maximum(value, 0.0) + jnp.log1p(jnp.exp(-jnp.abs(value)))
    dt = jnp.where(live, soft, 0.0)
    la = -jnp.exp(alog_ref[...]) * dt
    tri = (
        lax.broadcasted_iota(jnp.int32, (rows, rows), 0)
        >= lax.broadcasted_iota(jnp.int32, (rows, rows), 1)
    )
    tri = jnp.where(tri, 1.0, 0.0).astype(BF16)
    high = la.astype(BF16)
    rest = la - high.astype(F32)
    mid = rest.astype(BF16)
    low = (rest - mid.astype(F32)).astype(BF16)
    cum = (
        jnp.dot(tri, low, preferred_element_type=F32)
        + jnp.dot(tri, mid, preferred_element_type=F32)
        + jnp.dot(tri, high, preferred_element_type=F32)
    )
    last = cum[rows - 1 :, :]
    cum_ref[...] = cum
    some = dt > 0.0
    log_dt = jnp.where(some, jnp.log(jnp.where(some, dt, 1.0)), -1e30)
    shift_ref[...] = (cum - log_dt).T
    ending_ref[...] = jnp.exp(last - cum) * dt
    decay_ref[...] = jnp.broadcast_to(jnp.exp(last), decay_ref.shape)


def step_tables(at, dt_raw, dt_bias, a_log):
    _, rows, heads = dt_raw.shape
    whole = lambda *shape: pl.BlockSpec(shape, lambda i, a: (0,) * len(shape))
    return pl.pallas_call(
        steps_body,
        out_shape=(
            jax.ShapeDtypeStruct((rows, heads), F32),
            jax.ShapeDtypeStruct((heads, rows), F32),
            jax.ShapeDtypeStruct((rows, heads), F32),
            jax.ShapeDtypeStruct((8, heads), F32),
        ),
        grid_spec=pltpu.PrefetchScalarGridSpec(
            num_scalar_prefetch=1,
            grid=(1,),
            in_specs=[whole(1, rows, heads), whole(1, heads), whole(1, heads)],
            out_specs=[whole(rows, heads), whole(heads, rows), whole(rows, heads), whole(8, heads)],
        ),
        cost_estimate=cost(rows * rows * heads * 6, rows * heads * 16, rows * heads * 4),
        name="step_tables",
    )(at, dt_raw, dt_bias[None], a_log[None])


def pair_columns(table, p, first):
    rows = table.shape[0]
    left = jnp.broadcast_to(table[:, 2 * p : 2 * p + 1], (rows, LANES))
    right = jnp.broadcast_to(table[:, 2 * p + 1 : 2 * p + 2], (rows, LANES))
    return left, right, jnp.where(first, left, right)


def group_heads(ref, group, per_group):
    heads = ref.shape[1]
    return pltpu.roll(ref[...], lax.rem(heads - group * per_group, heads), 1)


def conv_body(
    at_ref, x_ref, b_ref, c_ref, rx_ref, rb_ref, rc_ref, wx_ref, wb_ref, wc_ref,
    bx_ref, bb_ref, bc_ref, ending_ref, xa_ref, ba_ref, ca_ref, state_ref, rows_ref, cols_ref,
):
    group = at_ref[0] + pl.program_id(0)
    rows = x_ref.shape[1]
    pairs = x_ref.shape[2] // LANES
    taps = wx_ref.shape[0]
    first = lax.broadcasted_iota(jnp.int32, (rows, LANES), 1) < LANES // 2
    cols_ref[...] = group_heads(ending_ref, group, 2 * pairs)

    def conv(slot, src, rim, weight, bias, at):
        lanes = slice(at, at + LANES)
        rows_ref[slot, 0:8] = rim[:, lanes]
        rows_ref[slot, 8 : 8 + rows] = src[0, :, lanes].astype(F32)
        total = bias[:, lanes]
        for k in range(taps):
            begin = 9 - taps + k
            total = total + weight[k : k + 1, lanes] * rows_ref[slot, begin : begin + rows]
        return silu(total).astype(BF16)

    b_act = conv(0, b_ref, rb_ref, wb_ref, bb_ref, 0)
    ba_ref[...] = b_act
    ca_ref[...] = conv(1, c_ref, rc_ref, wc_ref, bc_ref, 0)
    for p in range(pairs):
        act = conv(p % 2, x_ref, rx_ref, wx_ref, bx_ref, p * LANES)
        xa_ref[:, p * LANES : (p + 1) * LANES] = act
        _, _, ending = pair_columns(cols_ref, p, first)
        scaled = (act.astype(F32) * ending).astype(BF16)
        state = lax.dot_general(
            scaled, ba_ref[...], (((0,), (0,)), ((), ())), preferred_element_type=F32
        )
        state_ref[p * LANES : (p + 1) * LANES, :] = state.astype(BF16)


def conv_half(at, tokens, rim, weight, bias, ending, inner, nstate):
    _, rows, channels = tokens.shape
    heads = ending.shape[1]
    width = inner // GROUPS
    half = GROUPS // 2
    b_at, c_at = inner // nstate, inner // nstate + GROUPS
    taps = weight.shape[0]

    def three(lead):
        pre = (0,) * len(lead)
        return [
            pl.BlockSpec(lead + (width,), lambda i, a: pre + (a[0] + i,)),
            pl.BlockSpec(lead + (nstate,), lambda i, a: pre + (b_at + a[0] + i,)),
            pl.BlockSpec(lead + (nstate,), lambda i, a: pre + (c_at + a[0] + i,)),
        ]

    return pl.pallas_call(
        conv_body,
        out_shape=(
            jax.ShapeDtypeStruct((rows, half * width), BF16),
            jax.ShapeDtypeStruct((rows, half * nstate), BF16),
            jax.ShapeDtypeStruct((rows, half * nstate), BF16),
            jax.ShapeDtypeStruct((half * width, nstate), BF16),
        ),
        grid_spec=pltpu.PrefetchScalarGridSpec(
            num_scalar_prefetch=1,
            grid=(half,),
            in_specs=three((1, rows))
            + three((8,))
            + three((taps,))
            + three((1,))
            + [pl.BlockSpec((rows, heads), lambda i, a: (0, 0))],
            out_specs=[
                pl.BlockSpec((rows, width), lambda i, a: (0, i)),
                pl.BlockSpec((rows, nstate), lambda i, a: (0, i)),
                pl.BlockSpec((rows, nstate), lambda i, a: (0, i)),
                pl.BlockSpec((width, nstate), lambda i, a: (i, 0)),
            ],
            scratch_shapes=[pltpu.VMEM((2, rows + 8, LANES), F32), pltpu.VMEM((rows, heads), F32)],
        ),
        cost_estimate=cost(rows * channels * 40, rows * channels * 2, rows * channels // 2),
        name="conv_half",
    )(at, tokens, tokens, tokens, rim, rim, rim, weight, weight, weight, bias, bias, bias, ending)


def outbound_body(owner_ref, own_w_ref, recv_w_ref, own_ref, recv_ref, out_ref):
    step = pl.program_id(0)
    chunk = own_ref.shape[0]
    for k in range(chunk):
        page = step * chunk + k
        total = own_w_ref[page] * own_ref[k].astype(F32) + recv_w_ref[page] * recv_ref[k].astype(F32)
        out_ref[owner_ref[page]] = total.astype(BF16)


def outbound_pages(owners, own_w, recv_w, own, recv, devices):
    pages, rows, width = own.shape
    chunk = min(16, pages)
    return pl.pallas_call(
        outbound_body,
        out_shape=jax.ShapeDtypeStruct((devices, rows, width), BF16),
        grid_spec=pltpu.PrefetchScalarGridSpec(
            num_scalar_prefetch=3,
            grid=(pages // chunk,),
            in_specs=[pl.BlockSpec((chunk, rows, width), lambda i, *s: (i, 0, 0))] * 2,
            out_specs=pl.BlockSpec((devices, rows, width), lambda i, *s: (0, 0, 0)),
        ),
        cost_estimate=cost(pages * rows * width * 3, pages * rows * width * 8),
        name="outbound_pages",
    )(owners, own_w, recv_w, own, recv)


def start_body(owner_ref, decay_ref, at_ref, keep_ref, in_ref, own_ref, recv_ref, start_ref, send_ref):
    step = pl.program_id(0)
    chunk = own_ref.shape[0]
    keep = keep_ref[0]

    @pl.when(at_ref[0] == 0)
    def _():
        for k in range(chunk):
            page = step * chunk + k
            held = in_ref[owner_ref[page]].astype(F32) * keep
            start_ref[k] = held.astype(BF16)
            send_ref[k] = (decay_ref[page] * held + own_ref[k].astype(F32)).astype(BF16)

    @pl.when(at_ref[0] != 0)
    def _():
        for k in range(chunk):
            page = step * chunk + k
            held = in_ref[owner_ref[page]].astype(F32) * keep
            send_ref[k] = held.astype(BF16)
            start_ref[k] = (decay_ref[page] * held + recv_ref[k].astype(F32)).astype(BF16)


def start_states(owners, decay, ctx, keep, incoming, own, recv):
    pages, rows, width = own.shape
    chunk = min(16, pages)
    block = pl.BlockSpec((chunk, rows, width), lambda i, *s: (i, 0, 0))
    return pl.pallas_call(
        start_body,
        out_shape=(jax.ShapeDtypeStruct(own.shape, BF16),) * 2,
        grid_spec=pltpu.PrefetchScalarGridSpec(
            num_scalar_prefetch=4,
            grid=(pages // chunk,),
            in_specs=[pl.BlockSpec(incoming.shape, lambda i, *s: (0, 0, 0)), block, block],
            out_specs=[block, block],
        ),
        cost_estimate=cost(pages * rows * width * 4, pages * rows * width * 12),
        name="start_states",
    )(owners, decay, ctx, keep, incoming, own, recv)


def mixer_body(
    at_ref, x_ref, b_ref, c_ref, cum_ref, shift_ref, start_ref, gate_ref, skip_ref, norm_ref, *rest
):
    out_ref, cols_ref, score_ref, gated_ref = rest[-4:]
    group = at_ref[0] + pl.program_id(0)
    rows, width = x_ref.shape
    pairs = width // LANES
    half = rows // 2
    first = lax.broadcasted_iota(jnp.int32, (rows, LANES), 1) < LANES // 2
    cols_ref[...] = group_heads(cum_ref, group, 2 * pairs)
    b_val, c_val = b_ref[...], c_ref[...]
    nt = (((1,), (1,)), ((), ()))
    scores = lax.dot_general(c_val, b_val, nt, preferred_element_type=F32)
    lower = (
        lax.broadcasted_iota(jnp.int32, (rows, rows), 0)
        >= lax.broadcasted_iota(jnp.int32, (rows, rows), 1)
    )
    score_ref[...] = jnp.where(lower, scores, 0.0)
    squares = jnp.zeros((rows, LANES), F32)
    for p in range(pairs):
        lanes = slice(p * LANES, (p + 1) * LANES)
        x_val = x_ref[:, lanes]
        left, right, both = pair_columns(cols_ref, p, first)
        ys = []
        for cum, h in ((left, 2 * p), (right, 2 * p + 1)):
            early = shift_ref[h : h + 1, :half]
            late = shift_ref[h : h + 1, half:]
            w00 = score_ref[:half, :half] * jnp.exp(jnp.minimum(cum[:half] - early, TOP))
            w10 = score_ref[half:, :half] * jnp.exp(cum[half:] - early)
            w11 = score_ref[half:, half:] * jnp.exp(jnp.minimum(cum[half:] - late, TOP))
            y0 = jnp.dot(w00.astype(BF16), x_val[:half], preferred_element_type=F32)
            w1 = jnp.concatenate([w10.astype(BF16), w11.astype(BF16)], axis=1)
            y1 = jnp.dot(w1, x_val, preferred_element_type=F32)
            ys.append(jnp.concatenate([y0, y1], axis=0))
        carried = lax.dot_general(c_val, start_ref[lanes, :], nt, preferred_element_type=F32)
        y = jnp.where(first, ys[0], ys[1]) + jnp.exp(both) * carried
        y = y + skip_ref[:, lanes] * x_val.astype(F32)
        gated = y * silu(gate_ref[0, :, lanes].astype(F32))
        gated_ref[p] = gated
        squares = squares + gated * gated
    mean = jnp.sum(squares, axis=1, keepdims=True) * (1.0 / width)
    live = at_ref[1] + lax.broadcasted_iota(jnp.int32, (rows, 1), 0) < at_ref[2]
    factor = jnp.where(live, lax.rsqrt(mean + 1e-05), 0.0)
    factor = jnp.broadcast_to(factor, (rows, LANES))
    for p in range(pairs):
        lanes = slice(p * LANES, (p + 1) * LANES)
        out_ref[0, :, lanes] = (gated_ref[p] * factor * norm_ref[:, lanes]).astype(BF16)


def mixer_half(at, x, b, c, cum, shift, start, gate, skip, norm, so_far):
    rows, half_width = x.shape
    heads = cum.shape[1]
    half = GROUPS // 2
    width = half_width // half
    nstate = start.shape[1]
    per_group = heads // GROUPS
    in_specs = [
        pl.BlockSpec((rows, width), lambda i, a: (0, i)),
        pl.BlockSpec((rows, nstate), lambda i, a: (0, i)),
        pl.BlockSpec((rows, nstate), lambda i, a: (0, i)),
        pl.BlockSpec((rows, heads), lambda i, a: (0, 0)),
        pl.BlockSpec((per_group, rows), lambda i, a: (a[0] + i, 0)),
        pl.BlockSpec((width, nstate), lambda i, a: (i, 0)),
        pl.BlockSpec((1, rows, width), lambda i, a: (0, 0, a[0] + i)),
        pl.BlockSpec((1, width), lambda i, a: (0, a[0] + i)),
        pl.BlockSpec((1, width), lambda i, a: (0, a[0] + i)),
    ]
    args = [at, x, b, c, cum, shift, start, gate, skip, norm]
    aliases = {}
    if so_far is not None:
        in_specs.append(pl.BlockSpec(memory_space=pl.ANY))
        aliases = {len(args): 0}
        args.append(so_far)
    return pl.pallas_call(
        mixer_body,
        out_shape=jax.ShapeDtypeStruct(gate.shape, BF16),
        grid_spec=pltpu.PrefetchScalarGridSpec(
            num_scalar_prefetch=1,
            grid=(half,),
            in_specs=in_specs,
            out_specs=pl.BlockSpec((1, rows, width), lambda i, a: (0, 0, a[0] + i)),
            scratch_shapes=[
                pltpu.VMEM((rows, heads), F32),
                pltpu.VMEM((rows, rows), F32),
                pltpu.VMEM((width // LANES, rows, LANES), F32),
            ],
        ),
        input_output_aliases=aliases,
        cost_estimate=cost(
            rows * half_width * (2 * rows + 2 * nstate), rows * half_width * 8, rows * rows * heads // 2
        ),
        name="mixer_half",
    )(*args)


def pool_body(dev_ref, decay_ref, pool_ref, in_ref, out_ref):
    step = pl.program_id(0)
    chunk = pool_ref.shape[0]
    for k in range(chunk):
        slot = step * chunk + k
        device = dev_ref[slot]

        @pl.when(device >= 0)
        def _():
            out_ref[k] = decay_ref[slot] * pool_ref[k] + in_ref[device].astype(F32)

        @pl.when(device < 0)
        def _():
            out_ref[k] = pool_ref[k]


def updated_pool(dev_of_slot, decay, pool, returned):
    slots, rows, width = pool.shape
    chunk = min(32, slots)
    block = pl.BlockSpec((chunk, rows, width), lambda i, *s: (i, 0, 0))
    return pl.pallas_call(
        pool_body,
        out_shape=jax.ShapeDtypeStruct(pool.shape, F32),
        grid_spec=pltpu.PrefetchScalarGridSpec(
            num_scalar_prefetch=2,
            grid=(slots // chunk,),
            in_specs=[block, pl.BlockSpec(returned.shape, lambda i, *s: (0, 0, 0))],
            out_specs=block,
        ),
        cost_estimate=cost(slots * rows * width * 2, slots * rows * width * 10),
        name="updated_pool",
    )(dev_of_slot, decay, pool, returned)


def local(
    conv_input,
    gate_input,
    dt_raw,
    conv_weight,
    conv_bias,
    dt_bias,
    a_log,
    d_skip,
    norm_weight,
    conv_cache,
    state_pool,
    page_owner,
    page_slot,
    prefix_len,
    new_count,
):
    ctx_count = lax.axis_size("ctx")
    devices = lax.axis_size("req") * ctx_count
    req_index = lax.axis_index("req")
    ctx_index = lax.axis_index("ctx")
    own_index = req_index * ctx_count + ctx_index
    rows = conv_input.shape[1]
    heads = dt_raw.shape[2]
    inner = gate_input.shape[2]
    width = inner // heads
    slots, page_rows, nstate = state_pool.shape
    pages = page_owner.shape[1] // ctx_count
    rim = conv_weight.shape[0] - 1
    half_groups = GROUPS // 2

    owner_table = page_owner.reshape(devices, pages)
    slot_table = page_slot.reshape(devices, pages)
    matches = owner_table == own_index
    slot_for = jnp.max(jnp.where(matches, slot_table, -1), axis=1)
    dev_ids = jnp.arange(devices, dtype=jnp.int32)
    slot_hits = slot_for[None, :] == jnp.arange(slots, dtype=jnp.int32)[:, None]
    dev_of_slot = jnp.max(jnp.where(slot_hits, dev_ids[None, :], -1), axis=1)
    outgoing = gather_pages(dev_of_slot, state_pool, devices)
    incoming = lax.all_to_all(outgoing, ("req", "ctx"), split_axis=0, concat_axis=0, tiled=True)

    prefix = prefix_len[req_index]
    count = new_count[req_index]
    owners = owner_table[own_index]
    base = (ctx_index * rows).astype(jnp.int32)
    at = jnp.stack([base, count])
    cum, shift, ending, decay_rows = step_tables(at, dt_raw, dt_bias, a_log)
    decay = decay_rows[0:1]
    other_decay = swapped(decay)

    previous = lax.ppermute(conv_input[0, rows - rim :], "ctx", [(0, 1)])
    keep_rows = jnp.arange(rim) >= rim - prefix
    cached = jnp.where(keep_rows[:, None], conv_cache[0], jnp.zeros_like(conv_cache[0]))
    rim_rows = jnp.where(ctx_index == 0, cached, previous).astype(F32)
    rim_rows = jnp.concatenate([jnp.zeros((8 - rim, rim_rows.shape[1]), F32), rim_rows], axis=0)

    own_at = jnp.stack([ctx_index * half_groups, base, count]).astype(jnp.int32)
    other_at = jnp.stack([(1 - ctx_index) * half_groups, base, count]).astype(jnp.int32)
    conv_args = (conv_input, rim_rows, conv_weight, conv_bias[None], ending, inner, nstate)
    x_other, b_other, c_other, state_other = conv_half(other_at, *conv_args)
    received = swapped(state_other)
    x_own, b_own, c_own, state_own = conv_half(own_at, *conv_args)

    ctx_first = ctx_index == 0
    mine = jnp.where(ctx_first, decay[0, : heads // 2], decay[0, heads // 2 :])
    theirs = jnp.where(ctx_first, other_decay[0, : heads // 2], other_decay[0, heads // 2 :])
    decay_early = jnp.where(ctx_first, mine, theirs)
    decay_late = jnp.where(ctx_first, theirs, mine)
    ones = jnp.ones_like(mine)
    own_w = jnp.where(ctx_first, decay_late, ones)
    recv_w = jnp.where(ctx_first, ones, decay_late)
    as_pages = lambda value: value.reshape(pages, page_rows, nstate)
    own_pages, recv_pages = as_pages(state_own), as_pages(received)
    outbound = outbound_pages(owners, own_w, recv_w, own_pages, recv_pages, devices)
    returned = lax.all_to_all(outbound, ("req", "ctx"), split_axis=0, concat_axis=0, tiled=True)
    all_decays = lax.all_gather((mine * theirs)[None], ("req", "ctx"), axis=0, tiled=True)

    keep = (prefix > 0).astype(F32)[None]
    start, send = start_states(
        owners, decay_early, ctx_index[None].astype(jnp.int32), keep, incoming, own_pages, recv_pages
    )
    start_other = swapped(send)
    skip = jnp.repeat(d_skip, width)[None]
    norm = norm_weight[None]
    as_rows = lambda value: value.reshape(pages * page_rows, nstate)
    mixed = mixer_half(
        own_at, x_own, b_own, c_own, cum, shift, as_rows(start), gate_input, skip, norm, None
    )
    mixed = mixer_half(
        other_at, x_other, b_other, c_other, cum, shift, as_rows(start_other), gate_input, skip, norm, mixed
    )

    targets = count - rim + jnp.arange(rim)
    positions = base + jnp.arange(rows)
    picks = (positions[None, :] == targets[:, None]).astype(BF16)
    tail_rows = jnp.dot(picks, conv_input[0], preferred_element_type=F32).astype(BF16)
    new_tail = tail_rows + swapped(tail_rows)

    request_kept = jnp.repeat((prefix_len > 0).astype(F32), ctx_count)
    page_decay = jnp.sum(jnp.where(matches, all_decays, 0.0), axis=1) * request_kept
    slot_decay = jnp.sum(jnp.where(slot_hits, page_decay[None, :], 0.0), axis=1)
    new_pool = updated_pool(dev_of_slot, slot_decay, state_pool, returned)
    return (mixed, new_tail[None], new_pool)


def solution(mesh):
    return jax.shard_map(
        local,
        mesh=mesh,
        in_specs=(
            P("req", "ctx", None),
            P("req", "ctx", None),
            P("req", "ctx", None),
            P(),
            P(),
            P(),
            P(),
            P(),
            P(),
            P("req", None, None),
            P(("req", "ctx"), None, None),
            P(),
            P(),
            P(),
            P(),
        ),
        out_specs=(P("req", "ctx", None), P("req", None, None), P(("req", "ctx"), None, None)),
        check_vma=False,
    )
```

```python
import functools

import jax
import jax.numpy as jnp
from jax import lax
from jax.experimental import pallas as pl
from jax.experimental.pallas import tpu as pltpu
from jax.sharding import PartitionSpec as P

GROUPS = 8
LANES = 128
TAIL = 8
TOP = 88.72
F32 = jnp.float32
BF16 = jnp.bfloat16


def swapped(value):
    return lax.ppermute(value, "ctx", [(0, 1), (1, 0)])


def silu(value):
    half = 0.5 * value
    return half + half * jnp.tanh(half)


def cost(flops, nbytes, trans=0):
    return pl.CostEstimate(flops=flops, bytes_accessed=nbytes, transcendentals=trans)


def gather_body(dev_ref, pool_ref, out_ref):
    step = pl.program_id(0)
    for k in range(pool_ref.shape[0]):
        device = dev_ref[step * pool_ref.shape[0] + k]

        @pl.when(device >= 0)
        def _():
            out_ref[device] = pool_ref[k].astype(BF16)


def gather_pages(dev_of_slot, pool, devices):
    slots, rows, width = pool.shape
    chunk = min(32, slots)
    return pl.pallas_call(
        gather_body,
        out_shape=jax.ShapeDtypeStruct((devices, rows, width), BF16),
        grid_spec=pltpu.PrefetchScalarGridSpec(
            num_scalar_prefetch=1,
            grid=(slots // chunk,),
            in_specs=[pl.BlockSpec((chunk, rows, width), lambda i, d: (i, 0, 0))],
            out_specs=pl.BlockSpec((devices, rows, width), lambda i, d: (0, 0, 0)),
        ),
        cost_estimate=cost(slots * rows * width, slots * rows * width * 6),
        name="gather_pages",
    )(dev_of_slot, pool)


def steps_body(id_ref, count_ref, raw_ref, bias_ref, alog_ref, cum_ref, shift_ref, ending_ref, decay_ref):
    rows, heads = cum_ref.shape
    pos = id_ref[1] * rows + lax.broadcasted_iota(jnp.int32, (rows, heads), 0)
    live = pos < count_ref[id_ref[0]]
    value = raw_ref[0].astype(F32) + bias_ref[...]
    soft = jnp.maximum(value, 0.0) + jnp.log1p(jnp.exp(-jnp.abs(value)))
    dt = jnp.where(live, soft, 0.0)
    la = -jnp.exp(alog_ref[...]) * dt
    tri = (
        lax.broadcasted_iota(jnp.int32, (rows, rows), 0)
        >= lax.broadcasted_iota(jnp.int32, (rows, rows), 1)
    )
    tri = jnp.where(tri, 1.0, 0.0).astype(BF16)
    high = la.astype(BF16)
    rest = la - high.astype(F32)
    mid = rest.astype(BF16)
    low = (rest - mid.astype(F32)).astype(BF16)
    cum = (
        jnp.dot(tri, low, preferred_element_type=F32)
        + jnp.dot(tri, mid, preferred_element_type=F32)
        + jnp.dot(tri, high, preferred_element_type=F32)
    )
    last = cum[rows - 1 :, :]
    cum_ref[...] = cum
    some = dt > 0.0
    log_dt = jnp.where(some, jnp.log(jnp.where(some, dt, 1.0)), -1e30)
    shift_ref[...] = (cum - log_dt).T
    ending_ref[...] = jnp.exp(last - cum) * dt
    decay_ref[...] = jnp.broadcast_to(jnp.exp(last), decay_ref.shape)


def step_tables(ids, counts, dt_raw, dt_bias, a_log):
    _, rows, heads = dt_raw.shape
    whole = lambda *shape: pl.BlockSpec(shape, lambda i, *s: (0,) * len(shape))
    return pl.pallas_call(
        steps_body,
        out_shape=(
            jax.ShapeDtypeStruct((rows, heads), F32),
            jax.ShapeDtypeStruct((heads, rows), F32),
            jax.ShapeDtypeStruct((rows, heads), F32),
            jax.ShapeDtypeStruct((8, heads), F32),
        ),
        grid_spec=pltpu.PrefetchScalarGridSpec(
            num_scalar_prefetch=2,
            grid=(1,),
            in_specs=[whole(1, rows, heads), whole(1, heads), whole(1, heads)],
            out_specs=[whole(rows, heads), whole(heads, rows), whole(rows, heads), whole(8, heads)],
        ),
        cost_estimate=cost(rows * rows * heads * 6, rows * heads * 16, rows * heads * 4),
        name="step_tables",
    )(ids, counts, dt_raw, dt_bias[None], a_log[None])


def pair_columns(table, p, first):
    rows = table.shape[0]
    left = jnp.broadcast_to(table[:, 2 * p : 2 * p + 1], (rows, LANES))
    right = jnp.broadcast_to(table[:, 2 * p + 1 : 2 * p + 2], (rows, LANES))
    return left, right, jnp.where(first, left, right)


def first_group(id_ref, own):
    ctx = id_ref[1]
    return (ctx if own else 1 - ctx) * (GROUPS // 2)


def group_heads(ref, group, per_group):
    heads = ref.shape[1]
    return pltpu.roll(ref[...], lax.rem(heads - group * per_group, heads), 1)


def conv_body(
    own, id_ref, prefix_ref, x_ref, b_ref, c_ref, kx_ref, kb_ref, kc_ref, px_ref, pb_ref, pc_ref,
    wx_ref, wb_ref, wc_ref, bx_ref, bb_ref, bc_ref, ending_ref, xa_ref, ba_ref, ca_ref, state_ref, rows_ref, cols_ref,
):
    group = first_group(id_ref, own) + pl.program_id(0)
    rows = x_ref.shape[1]
    pairs = x_ref.shape[2] // LANES
    taps = wx_ref.shape[0]
    first = lax.broadcasted_iota(jnp.int32, (rows, LANES), 1) < LANES // 2
    cols_ref[...] = group_heads(ending_ref, group, 2 * pairs)

    held = lax.broadcasted_iota(jnp.int32, (taps - 1, LANES), 0) >= taps - 1 - prefix_ref[id_ref[0]]
    lead = id_ref[1] == 0

    def conv(slot, src, kept, before, weight, bias, at):
        lanes = slice(at, at + LANES)
        cached = jnp.where(held, kept[0, :, lanes].astype(F32), 0.0)
        rim = jnp.where(lead, cached, before[:, lanes].astype(F32))
        rows_ref[slot, 9 - taps : 8] = rim
        rows_ref[slot, 8 : 8 + rows] = src[0, :, lanes].astype(F32)
        total = bias[:, lanes]
        for k in range(taps):
            begin = 9 - taps + k
            total = total + weight[k : k + 1, lanes] * rows_ref[slot, begin : begin + rows]
        return silu(total).astype(BF16)

    b_act = conv(0, b_ref, kb_ref, pb_ref, wb_ref, bb_ref, 0)
    ba_ref[...] = b_act
    ca_ref[...] = conv(1, c_ref, kc_ref, pc_ref, wc_ref, bc_ref, 0)
    for p in range(pairs):
        act = conv(p % 2, x_ref, kx_ref, px_ref, wx_ref, bx_ref, p * LANES)
        xa_ref[:, p * LANES : (p + 1) * LANES] = act
        _, _, ending = pair_columns(cols_ref, p, first)
        scaled = (act.astype(F32) * ending).astype(BF16)
        state = lax.dot_general(
            scaled, ba_ref[...], (((0,), (0,)), ((), ())), preferred_element_type=F32
        )
        state_ref[p * LANES : (p + 1) * LANES, :] = state.astype(BF16)


def conv_half(own, ids, prefix, tokens, cache, before, weight, bias, ending, inner, nstate):
    _, rows, channels = tokens.shape
    heads = ending.shape[1]
    width = inner // GROUPS
    half = GROUPS // 2
    b_at, c_at = inner // nstate, inner // nstate + GROUPS
    taps = weight.shape[0]

    def three(lead):
        pre = (0,) * len(lead)
        return [
            pl.BlockSpec(lead + (width,), lambda i, a, b: pre + (first_group(a, own) + i,)),
            pl.BlockSpec(lead + (nstate,), lambda i, a, b: pre + (b_at + first_group(a, own) + i,)),
            pl.BlockSpec(lead + (nstate,), lambda i, a, b: pre + (c_at + first_group(a, own) + i,)),
        ]

    return pl.pallas_call(
        functools.partial(conv_body, own),
        out_shape=(
            jax.ShapeDtypeStruct((rows, half * width), BF16),
            jax.ShapeDtypeStruct((rows, half * nstate), BF16),
            jax.ShapeDtypeStruct((rows, half * nstate), BF16),
            jax.ShapeDtypeStruct((half * width, nstate), BF16),
        ),
        grid_spec=pltpu.PrefetchScalarGridSpec(
            num_scalar_prefetch=2,
            grid=(half,),
            in_specs=three((1, rows))
            + three((1, taps - 1))
            + three((taps - 1,))
            + three((taps,))
            + three((1,))
            + [pl.BlockSpec((rows, heads), lambda i, a, b: (0, 0))],
            out_specs=[
                pl.BlockSpec((rows, width), lambda i, a, b: (0, i)),
                pl.BlockSpec((rows, nstate), lambda i, a, b: (0, i)),
                pl.BlockSpec((rows, nstate), lambda i, a, b: (0, i)),
                pl.BlockSpec((width, nstate), lambda i, a, b: (i, 0)),
            ],
            scratch_shapes=[pltpu.VMEM((2, rows + 8, LANES), F32), pltpu.VMEM((rows, heads), F32)],
        ),
        cost_estimate=cost(rows * channels * 40, rows * channels * 2, rows * channels // 2),
        name="conv_half",
    )(ids, prefix, tokens, tokens, tokens, cache, cache, cache, before, before, before, weight, weight, weight, bias, bias, bias, ending)


def outbound_body(
    owner_ref, early_ref, late_ref, id_ref, prefix_ref, own_ref, recv_ref, out_ref
):
    step = pl.program_id(0)
    chunk, rows, width = own_ref.shape
    lead = id_ref[1] == 0
    keep = jnp.where(prefix_ref[id_ref[0]] > 0, 1.0, 0.0)
    top = lax.broadcasted_iota(jnp.int32, (TAIL, width), 0) == 0
    for k in range(chunk):
        page = step * chunk + k
        late = late_ref[page]
        own_w = jnp.where(lead, late, 1.0)
        recv_w = jnp.where(lead, 1.0, late)
        total = own_w * own_ref[k].astype(F32) + recv_w * recv_ref[k].astype(F32)
        whole = jnp.full((TAIL, width), early_ref[page] * late * keep, F32)
        high = whole.astype(BF16).astype(F32)
        owner = owner_ref[page]
        out_ref[owner, :rows] = total.astype(BF16)
        out_ref[owner, rows:] = jnp.where(top, high, whole - high).astype(BF16)


def outbound_pages(owners, early, late, ids, prefix, own, recv, devices):
    pages, rows, width = own.shape
    chunk = min(16, pages)
    return pl.pallas_call(
        outbound_body,
        out_shape=jax.ShapeDtypeStruct((devices, rows + TAIL, width), BF16),
        grid_spec=pltpu.PrefetchScalarGridSpec(
            num_scalar_prefetch=5,
            grid=(pages // chunk,),
            in_specs=[pl.BlockSpec((chunk, rows, width), lambda i, *s: (i, 0, 0))] * 2,
            out_specs=pl.BlockSpec((devices, rows + TAIL, width), lambda i, *s: (0, 0, 0)),
        ),
        cost_estimate=cost(pages * rows * width * 3, pages * rows * width * 8),
        name="outbound_pages",
    )(owners, early, late, ids, prefix, own, recv)


def start_body(owner_ref, decay_ref, id_ref, prefix_ref, in_ref, own_ref, recv_ref, start_ref, send_ref):
    step = pl.program_id(0)
    chunk = own_ref.shape[0]
    keep = jnp.where(prefix_ref[id_ref[0]] > 0, 1.0, 0.0)

    @pl.when(id_ref[1] == 0)
    def _():
        for k in range(chunk):
            page = step * chunk + k
            held = in_ref[owner_ref[page]].astype(F32) * keep
            start_ref[k] = held.astype(BF16)
            send_ref[k] = (decay_ref[page] * held + own_ref[k].astype(F32)).astype(BF16)

    @pl.when(id_ref[1] != 0)
    def _():
        for k in range(chunk):
            page = step * chunk + k
            held = in_ref[owner_ref[page]].astype(F32) * keep
            send_ref[k] = held.astype(BF16)
            start_ref[k] = (decay_ref[page] * held + recv_ref[k].astype(F32)).astype(BF16)


def start_states(owners, decay, ids, prefix, incoming, own, recv):
    pages, rows, width = own.shape
    chunk = min(16, pages)
    block = pl.BlockSpec((chunk, rows, width), lambda i, *s: (i, 0, 0))
    return pl.pallas_call(
        start_body,
        out_shape=(jax.ShapeDtypeStruct(own.shape, BF16),) * 2,
        grid_spec=pltpu.PrefetchScalarGridSpec(
            num_scalar_prefetch=4,
            grid=(pages // chunk,),
            in_specs=[pl.BlockSpec(incoming.shape, lambda i, *s: (0, 0, 0)), block, block],
            out_specs=[block, block],
        ),
        cost_estimate=cost(pages * rows * width * 4, pages * rows * width * 12),
        name="start_states",
    )(owners, decay, ids, prefix, incoming, own, recv)


def mixer_body(
    own, id_ref, count_ref, skip_ref, x_ref, b_ref, c_ref, cum_ref, shift_ref, start_ref, gate_ref,
    norm_ref, *rest
):
    out_ref, cols_ref, score_ref, gated_ref = rest[-4:]
    group = first_group(id_ref, own) + pl.program_id(0)
    rows, width = x_ref.shape
    pairs = width // LANES
    half = rows // 2
    first = lax.broadcasted_iota(jnp.int32, (rows, LANES), 1) < LANES // 2
    cols_ref[...] = group_heads(cum_ref, group, 2 * pairs)
    b_val, c_val = b_ref[...], c_ref[...]
    nt = (((1,), (1,)), ((), ()))
    scores = lax.dot_general(c_val, b_val, nt, preferred_element_type=F32)
    lower = (
        lax.broadcasted_iota(jnp.int32, (rows, rows), 0)
        >= lax.broadcasted_iota(jnp.int32, (rows, rows), 1)
    )
    score_ref[...] = jnp.where(lower, scores, 0.0)
    squares = jnp.zeros((rows, LANES), F32)
    for p in range(pairs):
        lanes = slice(p * LANES, (p + 1) * LANES)
        x_val = x_ref[:, lanes]
        left, right, both = pair_columns(cols_ref, p, first)
        ys = []
        for cum, h in ((left, 2 * p), (right, 2 * p + 1)):
            early = shift_ref[h : h + 1, :half]
            late = shift_ref[h : h + 1, half:]
            w00 = score_ref[:half, :half] * jnp.exp(jnp.minimum(cum[:half] - early, TOP))
            w10 = score_ref[half:, :half] * jnp.exp(cum[half:] - early)
            w11 = score_ref[half:, half:] * jnp.exp(jnp.minimum(cum[half:] - late, TOP))
            y0 = jnp.dot(w00.astype(BF16), x_val[:half], preferred_element_type=F32)
            w1 = jnp.concatenate([w10.astype(BF16), w11.astype(BF16)], axis=1)
            y1 = jnp.dot(w1, x_val, preferred_element_type=F32)
            ys.append(jnp.concatenate([y0, y1], axis=0))
        carried = lax.dot_general(c_val, start_ref[lanes, :], nt, preferred_element_type=F32)
        y = jnp.where(first, ys[0], ys[1]) + jnp.exp(both) * carried
        head = group * 2 * pairs + 2 * p
        skip = jnp.where(first, skip_ref[head], skip_ref[head + 1])
        y = y + skip * x_val.astype(F32)
        gated = y * silu(gate_ref[0, :, lanes].astype(F32))
        gated_ref[p] = gated
        squares = squares + gated * gated
    mean = jnp.sum(squares, axis=1, keepdims=True) * (1.0 / width)
    pos = id_ref[1] * rows + lax.broadcasted_iota(jnp.int32, (rows, 1), 0)
    live = pos < count_ref[id_ref[0]]
    factor = jnp.where(live, lax.rsqrt(mean + 1e-05), 0.0)
    factor = jnp.broadcast_to(factor, (rows, LANES))
    for p in range(pairs):
        lanes = slice(p * LANES, (p + 1) * LANES)
        out_ref[0, :, lanes] = (gated_ref[p] * factor * norm_ref[:, lanes]).astype(BF16)


def mixer_half(own, ids, counts, skip, x, b, c, cum, shift, start, gate, norm, so_far):
    rows, half_width = x.shape
    heads = cum.shape[1]
    half = GROUPS // 2
    width = half_width // half
    nstate = start.shape[1]
    per_group = heads // GROUPS
    in_specs = [
        pl.BlockSpec((rows, width), lambda i, a, *s: (0, i)),
        pl.BlockSpec((rows, nstate), lambda i, a, *s: (0, i)),
        pl.BlockSpec((rows, nstate), lambda i, a, *s: (0, i)),
        pl.BlockSpec((rows, heads), lambda i, a, *s: (0, 0)),
        pl.BlockSpec((per_group, rows), lambda i, a, *s: (first_group(a, own) + i, 0)),
        pl.BlockSpec((width, nstate), lambda i, a, *s: (i, 0)),
        pl.BlockSpec((1, rows, width), lambda i, a, *s: (0, 0, first_group(a, own) + i)),
        pl.BlockSpec((1, width), lambda i, a, *s: (0, first_group(a, own) + i)),
    ]
    args = [ids, counts, skip, x, b, c, cum, shift, start, gate, norm]
    aliases = {}
    if so_far is not None:
        in_specs.append(pl.BlockSpec(memory_space=pl.ANY))
        aliases = {len(args): 0}
        args.append(so_far)
    return pl.pallas_call(
        functools.partial(mixer_body, own),
        out_shape=jax.ShapeDtypeStruct(gate.shape, BF16),
        grid_spec=pltpu.PrefetchScalarGridSpec(
            num_scalar_prefetch=3,
            grid=(half,),
            in_specs=in_specs,
            out_specs=pl.BlockSpec((1, rows, width), lambda i, a, *s: (0, 0, first_group(a, own) + i)),
            scratch_shapes=[
                pltpu.VMEM((rows, heads), F32),
                pltpu.VMEM((rows, rows), F32),
                pltpu.VMEM((width // LANES, rows, LANES), F32),
            ],
        ),
        input_output_aliases=aliases,
        cost_estimate=cost(
            rows * half_width * (2 * rows + 2 * nstate), rows * half_width * 8, rows * rows * heads // 2
        ),
        name="mixer_half",
    )(*args)


def pool_body(dev_ref, pool_ref, in_ref, out_ref):
    step = pl.program_id(0)
    chunk, rows, _ = pool_ref.shape
    for k in range(chunk):
        slot = step * chunk + k
        device = dev_ref[slot]

        @pl.when(device >= 0)
        def _():
            tail = in_ref[device, rows:].astype(F32)
            whole = tail[0:1] + tail[1:2]
            out_ref[k] = whole * pool_ref[k] + in_ref[device, :rows].astype(F32)

        @pl.when(device < 0)
        def _():
            out_ref[k] = pool_ref[k]


def updated_pool(dev_of_slot, pool, returned):
    slots, rows, width = pool.shape
    chunk = min(32, slots)
    block = pl.BlockSpec((chunk, rows, width), lambda i, *s: (i, 0, 0))
    return pl.pallas_call(
        pool_body,
        out_shape=jax.ShapeDtypeStruct(pool.shape, F32),
        grid_spec=pltpu.PrefetchScalarGridSpec(
            num_scalar_prefetch=1,
            grid=(slots // chunk,),
            in_specs=[block, pl.BlockSpec(returned.shape, lambda i, *s: (0, 0, 0))],
            out_specs=block,
        ),
        cost_estimate=cost(slots * rows * width * 2, slots * rows * width * 10),
        name="updated_pool",
    )(dev_of_slot, pool, returned)


def local(
    conv_input,
    gate_input,
    dt_raw,
    conv_weight,
    conv_bias,
    dt_bias,
    a_log,
    d_skip,
    norm_weight,
    conv_cache,
    state_pool,
    page_owner,
    page_slot,
    prefix_len,
    new_count,
):
    ctx_count = lax.axis_size("ctx")
    devices = lax.axis_size("req") * ctx_count
    req_index = lax.axis_index("req")
    ctx_index = lax.axis_index("ctx")
    own_index = req_index * ctx_count + ctx_index
    rows = conv_input.shape[1]
    heads = dt_raw.shape[2]
    inner = gate_input.shape[2]
    slots, page_rows, nstate = state_pool.shape
    pages = page_owner.shape[1] // ctx_count
    rim = conv_weight.shape[0] - 1
    requests = page_owner.shape[0]

    matches = page_owner == own_index
    early = jnp.arange(2 * pages)[None, :] < pages
    slot_0 = jnp.max(jnp.where(matches & early, page_slot, -1), axis=1)
    slot_1 = jnp.max(jnp.where(matches & ~early, page_slot, -1), axis=1)
    slot_ids = jnp.arange(slots, dtype=jnp.int32)[:, None]
    request_ids = jnp.arange(requests, dtype=jnp.int32)[None, :]
    hits_0, hits_1 = slot_0[None, :] == slot_ids, slot_1[None, :] == slot_ids
    dev_of_slot = jnp.max(
        jnp.maximum(
            jnp.where(hits_0, 2 * request_ids, -1), jnp.where(hits_1, 2 * request_ids + 1, -1)
        ),
        axis=1,
    )
    outgoing = gather_pages(dev_of_slot, state_pool, devices)
    outgoing, conv_input, dt_raw, new_count, prefix_len, page_owner = lax.optimization_barrier(
        (outgoing, conv_input, dt_raw, new_count, prefix_len, page_owner)
    )
    incoming = lax.all_to_all(outgoing, ("req", "ctx"), split_axis=0, concat_axis=0, tiled=True)

    ids = jnp.stack([req_index, ctx_index]).astype(jnp.int32)
    owners = lax.dynamic_slice(page_owner, (req_index, ctx_index * pages), (1, pages))[0]
    previous = lax.ppermute(conv_input[0, rows - rim :], "ctx", [(0, 1)])
    cum, shift, ending, decay_rows = step_tables(ids, new_count, dt_raw, dt_bias, a_log)
    decay = decay_rows[0:1]
    other_decay = swapped(decay)

    conv_args = (
        ids, prefix_len, conv_input, conv_cache, previous, conv_weight, conv_bias[None], ending, inner, nstate
    )
    x_other, b_other, c_other, state_other = conv_half(False, *conv_args)
    received = swapped(state_other)
    x_own, b_own, c_own, state_own = conv_half(True, *conv_args)

    ctx_first = ctx_index == 0
    mine = jnp.where(ctx_first, decay[0, : heads // 2], decay[0, heads // 2 :])
    theirs = jnp.where(ctx_first, other_decay[0, : heads // 2], other_decay[0, heads // 2 :])
    decay_early = jnp.where(ctx_first, mine, theirs)
    decay_late = jnp.where(ctx_first, theirs, mine)
    as_pages = lambda value: value.reshape(pages, page_rows, nstate)
    own_pages, recv_pages = as_pages(state_own), as_pages(received)
    outbound = outbound_pages(
        owners, decay_early, decay_late, ids, prefix_len, own_pages, recv_pages, devices
    )
    returned = lax.all_to_all(outbound, ("req", "ctx"), split_axis=0, concat_axis=0, tiled=True)

    start, send = start_states(
        owners, decay_early, ids, prefix_len, incoming, own_pages, recv_pages
    )
    start_other = swapped(send)
    as_rows = lambda value: value.reshape(pages * page_rows, nstate)
    mixed = mixer_half(
        True, ids, new_count, d_skip, x_own, b_own, c_own, cum, shift, as_rows(start), gate_input,
        norm_weight[None], None,
    )
    mixed = mixer_half(
        False, ids, new_count, d_skip, x_other, b_other, c_other, cum, shift, as_rows(start_other),
        gate_input, norm_weight[None], mixed,
    )

    targets = new_count[req_index] - rim + jnp.arange(rim)
    positions = ctx_index * rows + jnp.arange(rows)
    picks = (positions[None, :] == targets[:, None]).astype(BF16)
    tail_rows = jnp.dot(picks, conv_input[0], preferred_element_type=F32).astype(BF16)
    new_tail = tail_rows + swapped(tail_rows)

    new_pool = updated_pool(dev_of_slot, state_pool, returned)
    return (mixed, new_tail[None], new_pool)


def solution(mesh):
    return jax.shard_map(
        local,
        mesh=mesh,
        in_specs=(
            P("req", "ctx", None),
            P("req", "ctx", None),
            P("req", "ctx", None),
            P(),
            P(),
            P(),
            P(),
            P(),
            P(),
            P("req", None, None),
            P(("req", "ctx"), None, None),
            P(),
            P(),
            P(),
            P(),
        ),
        out_specs=(P("req", "ctx", None), P("req", None, None), P(("req", "ctx"), None, None)),
        check_vma=False,
    )
```

```python
import functools

import jax
import jax.numpy as jnp
from jax import lax
from jax.experimental import pallas as pl
from jax.experimental.pallas import tpu as pltpu
from jax.sharding import PartitionSpec as P

GROUPS = 8
LANES = 128
TAIL = 8
PARTS = 4
GRANT = 64 << 20
TOP = 88.72
F32 = jnp.float32
IN_HBM = pl.BlockSpec(memory_space=pltpu.HBM)
BF16 = jnp.bfloat16


def swapped(value):
    return lax.ppermute(value, "ctx", [(0, 1), (1, 0)])


def silu(value):
    half = 0.5 * value
    return half + half * jnp.tanh(half)


def cost(flops, nbytes, trans=0):
    return pl.CostEstimate(flops=flops, bytes_accessed=nbytes, transcendentals=trans)


def part_copies(source, target, sems, parts):
    size = source.shape[0] // parts
    return [
        pltpu.make_async_copy(
            source.at[pl.ds(c * size, size)], target.at[pl.ds(c * size, size)], sems.at[c]
        )
        for c in range(parts)
    ]


def gather_body(early_ref, late_ref, pool_ref, out_ref, page_ref, round_ref, in_sem, out_sem):
    devices = round_ref.shape[0]
    ins = part_copies(pool_ref, page_ref, in_sem, PARTS)
    outs = part_copies(round_ref, out_ref, out_sem, PARTS)
    for copy in ins:
        copy.start()
    for copy in ins:
        copy.wait()
    for c in range(PARTS):
        for k in range(devices // PARTS):
            device = c * (devices // PARTS) + k
            slot = (early_ref, late_ref)[device % 2][device // 2]
            round_ref[device] = page_ref[jnp.maximum(slot, 0)].astype(BF16)
        outs[c].start()
    for copy in outs:
        copy.wait()


def gather_pages(slot_early, slot_late, pool, devices):
    slots, rows, width = pool.shape
    return pl.pallas_call(
        gather_body,
        out_shape=jax.ShapeDtypeStruct((devices, rows, width), BF16),
        grid_spec=pltpu.PrefetchScalarGridSpec(
            num_scalar_prefetch=2,
            grid=(1,),
            in_specs=[IN_HBM],
            out_specs=IN_HBM,
            scratch_shapes=[
                pltpu.VMEM((slots, rows, width), F32),
                pltpu.VMEM((devices, rows, width), BF16),
                pltpu.SemaphoreType.DMA((PARTS,)),
                pltpu.SemaphoreType.DMA((PARTS,)),
            ],
        ),
        compiler_params=pltpu.CompilerParams(vmem_limit_bytes=GRANT),
        cost_estimate=cost(slots * rows * width, slots * rows * width * 6),
        name="gather_pages",
    )(slot_early, slot_late, pool)


def steps_body(id_ref, count_ref, raw_ref, bias_ref, alog_ref, cum_ref, shift_ref, ending_ref, decay_ref):
    rows, heads = cum_ref.shape
    pos = id_ref[1] * rows + lax.broadcasted_iota(jnp.int32, (rows, heads), 0)
    live = pos < count_ref[id_ref[0]]
    value = raw_ref[0].astype(F32) + bias_ref[...]
    soft = jnp.maximum(value, 0.0) + jnp.log1p(jnp.exp(-jnp.abs(value)))
    dt = jnp.where(live, soft, 0.0)
    la = -jnp.exp(alog_ref[...]) * dt
    tri = (
        lax.broadcasted_iota(jnp.int32, (rows, rows), 0)
        >= lax.broadcasted_iota(jnp.int32, (rows, rows), 1)
    )
    tri = jnp.where(tri, 1.0, 0.0).astype(BF16)
    high = la.astype(BF16)
    rest = la - high.astype(F32)
    mid = rest.astype(BF16)
    low = (rest - mid.astype(F32)).astype(BF16)
    cum = (
        jnp.dot(tri, low, preferred_element_type=F32)
        + jnp.dot(tri, mid, preferred_element_type=F32)
        + jnp.dot(tri, high, preferred_element_type=F32)
    )
    last = cum[rows - 1 :, :]
    cum_ref[...] = cum
    some = dt > 0.0
    log_dt = jnp.where(some, jnp.log(jnp.where(some, dt, 1.0)), -1e30)
    shift_ref[...] = (cum - log_dt).T
    ending_ref[...] = jnp.exp(last - cum) * dt
    decay_ref[...] = jnp.broadcast_to(jnp.exp(last), decay_ref.shape)


def step_tables(ids, counts, dt_raw, dt_bias, a_log):
    _, rows, heads = dt_raw.shape
    whole = lambda *shape: pl.BlockSpec(shape, lambda i, *s: (0,) * len(shape))
    return pl.pallas_call(
        steps_body,
        out_shape=(
            jax.ShapeDtypeStruct((rows, heads), F32),
            jax.ShapeDtypeStruct((heads, rows), F32),
            jax.ShapeDtypeStruct((rows, heads), F32),
            jax.ShapeDtypeStruct((8, heads), F32),
        ),
        grid_spec=pltpu.PrefetchScalarGridSpec(
            num_scalar_prefetch=2,
            grid=(1,),
            in_specs=[whole(1, rows, heads), whole(1, heads), whole(1, heads)],
            out_specs=[whole(rows, heads), whole(heads, rows), whole(rows, heads), whole(8, heads)],
        ),
        compiler_params=pltpu.CompilerParams(vmem_limit_bytes=GRANT),
        cost_estimate=cost(rows * rows * heads * 6, rows * heads * 16, rows * heads * 4),
        name="step_tables",
    )(ids, counts, dt_raw, dt_bias[None], a_log[None])


def pair_columns(table, p, first):
    rows = table.shape[0]
    left = jnp.broadcast_to(table[:, 2 * p : 2 * p + 1], (rows, LANES))
    right = jnp.broadcast_to(table[:, 2 * p + 1 : 2 * p + 2], (rows, LANES))
    return left, right, jnp.where(first, left, right)


def first_group(id_ref, own):
    ctx = id_ref[1]
    return (ctx if own else 1 - ctx) * (GROUPS // 2)


def group_heads(ref, group, per_group):
    heads = ref.shape[1]
    return pltpu.roll(ref[...], lax.rem(heads - group * per_group, heads), 1)


def conv_body(
    own, channels, id_ref, prefix_ref, count_ref, x_ref, b_ref, c_ref, cache_ref, before_ref, weight_ref, bias_ref,
    ending_ref, *rest
):
    xa_ref, bc_ref, state_ref, tail_ref, rows_ref, cols_ref = rest[-6:]
    group = first_group(id_ref, own) + pl.program_id(0)
    rows = x_ref.shape[1]
    width = x_ref.shape[2]
    nstate = b_ref.shape[2]
    pairs = width // LANES
    taps = weight_ref.shape[0]
    b_at, c_at = channels
    first = lax.broadcasted_iota(jnp.int32, (rows, LANES), 1) < LANES // 2
    cols_ref[...] = group_heads(ending_ref, group, 2 * pairs)
    held = lax.broadcasted_iota(jnp.int32, (taps - 1, LANES), 0) >= taps - 1 - prefix_ref[id_ref[0]]
    lead = id_ref[1] == 0
    last = count_ref[id_ref[0]] - id_ref[1] * rows
    newest = 9 - taps + jnp.clip(last, 0, rows)
    if own:

        @pl.when(pl.program_id(0) == 0)
        def _():
            tail_ref[...] = rest[0][...]

    def conv(slot, src, at, begin):
        lanes = pl.ds(pl.multiple_of(begin, LANES), LANES)
        cached = jnp.where(held, cache_ref[0, :, lanes].astype(F32), 0.0)
        rim = jnp.where(lead, cached, before_ref[:, lanes].astype(F32))
        rows_ref[slot, 9 - taps : 8] = rim
        rows_ref[slot, 8 : 8 + rows] = src[0, :, at : at + LANES].astype(F32)
        tail_ref[:, lanes] = rows_ref[slot, pl.ds(newest, 8)].astype(BF16)
        total = bias_ref[:, lanes]
        weight = weight_ref[:, lanes]
        for k in range(taps):
            start = 9 - taps + k
            total = total + weight[k : k + 1] * rows_ref[slot, start : start + rows]
        return silu(total).astype(BF16)

    bc_ref[:, :nstate] = conv(0, b_ref, 0, b_at + group * nstate)
    bc_ref[:, nstate:] = conv(1, c_ref, 0, c_at + group * nstate)
    b_turned = bc_ref[:, :nstate].T
    nt = (((1,), (1,)), ((), ()))
    down = lax.broadcasted_iota(jnp.int32, (LANES, LANES), 0)
    across = lax.broadcasted_iota(jnp.int32, (LANES, LANES), 1)
    same = jnp.where(down == across, 1.0, 0.0).astype(BF16)
    for p in range(pairs):
        act = conv(p % 2, x_ref, p * LANES, group * width + p * LANES)
        xa_ref[:, p * LANES : (p + 1) * LANES] = act
        _, _, ending = pair_columns(cols_ref, p, first)
        scaled = (act.astype(F32) * ending).astype(BF16)
        turned = jnp.dot(b_turned, scaled, preferred_element_type=F32).astype(BF16)
        state = lax.dot_general(same, turned, nt, preferred_element_type=F32)
        state_ref[p * LANES : (p + 1) * LANES, :] = state.astype(BF16)


def conv_half(own, ids, prefix, counts, tail, tokens, cache, before, weight, bias, ending, inner, nstate):
    _, rows, channels = tokens.shape
    heads = ending.shape[1]
    width = inner // GROUPS
    half = GROUPS // 2
    b_at, c_at = inner, inner + GROUPS * nstate

    def channel_block(wide, begin):
        return pl.BlockSpec(
            (1, rows, wide), lambda i, a, *s: (0, 0, begin // wide + first_group(a, own) + i)
        )

    def whole(value):
        return pl.BlockSpec(value.shape, lambda i, *s: (0,) * value.ndim)

    tails = [] if tail is None else [tail]
    return pl.pallas_call(
        functools.partial(conv_body, own, (b_at, c_at)),
        out_shape=(
            jax.ShapeDtypeStruct((rows, half * width), BF16),
            jax.ShapeDtypeStruct((rows, half * 2 * nstate), BF16),
            jax.ShapeDtypeStruct((half * width, nstate), BF16),
            jax.ShapeDtypeStruct((8, channels), BF16),
        ),
        grid_spec=pltpu.PrefetchScalarGridSpec(
            num_scalar_prefetch=3,
            grid=(half,),
            in_specs=[
                channel_block(width, 0),
                channel_block(nstate, b_at),
                channel_block(nstate, c_at),
                whole(cache),
                whole(before),
                whole(weight),
                whole(bias),
                whole(ending),
            ]
            + [whole(value) for value in tails],
            out_specs=[
                pl.BlockSpec((rows, width), lambda i, *s: (0, i)),
                pl.BlockSpec((rows, 2 * nstate), lambda i, *s: (0, i)),
                pl.BlockSpec((width, nstate), lambda i, *s: (i, 0)),
                pl.BlockSpec((8, channels), lambda i, *s: (0, 0)),
            ],
            scratch_shapes=[pltpu.VMEM((2, rows + 16, LANES), F32), pltpu.VMEM((rows, heads), F32)],
        ),
        compiler_params=pltpu.CompilerParams(vmem_limit_bytes=GRANT),
        cost_estimate=cost(rows * channels * 40, rows * channels * 2, rows * channels // 2),
        name="conv_half",
    )(ids, prefix, counts, tokens, tokens, tokens, cache, before, weight, bias, ending, *tails)


def owner_of(owner_ref, id_ref, page, pages):
    return owner_ref[lax.rem(id_ref[0], owner_ref.shape[0]), id_ref[1] * pages + page]


def owner_block(owners):
    deep = min(8, owners.shape[0])
    return pl.BlockSpec(
        (deep, owners.shape[1]), lambda i, d, *s: (d[0] // deep, 0), memory_space=pltpu.SMEM
    )


def decay_block(decay):
    return pl.BlockSpec(decay.shape, lambda i, *s: (0, 0), memory_space=pltpu.SMEM)


def outbound_body(
    id_ref, prefix_ref, owner_ref, mine_ref, theirs_ref, own_hbm, recv_hbm, out_ref, own_ref, recv_ref,
    page_ref, own_sem, recv_sem, sem,
):
    pages, rows, width = own_ref.shape
    lead = id_ref[1] == 0
    keep = jnp.where(prefix_ref[id_ref[0]] > 0, 1.0, 0.0)
    top = lax.broadcasted_iota(jnp.int32, (TAIL, width), 0) == 0
    own_in = part_copies(own_hbm, own_ref, own_sem, PARTS)
    recv_in = part_copies(recv_hbm, recv_ref, recv_sem, PARTS)
    for c in range(PARTS):
        own_in[c].start()
        recv_in[c].start()
    outs = []
    for c in range(PARTS):
        own_in[c].wait()
        recv_in[c].wait()
        for k in range(pages // PARTS):
            page = c * (pages // PARTS) + k
            head = id_ref[1] * pages + page
            mine, theirs = mine_ref[0, head], theirs_ref[0, head]
            own_w = jnp.where(lead, theirs, 1.0)
            recv_w = jnp.where(lead, 1.0, mine)
            total = own_w * own_ref[page].astype(F32) + recv_w * recv_ref[page].astype(F32)
            whole = jnp.full((TAIL, width), mine * theirs * keep, F32)
            high = whole.astype(BF16).astype(F32)
            page_ref[page, :rows] = total.astype(BF16)
            page_ref[page, rows:] = jnp.where(top, high, whole - high).astype(BF16)
        for k in range(pages // PARTS):
            page = c * (pages // PARTS) + k
            owner = owner_of(owner_ref, id_ref, page, pages)
            copy = pltpu.make_async_copy(page_ref.at[page], out_ref.at[owner], sem.at[page])
            copy.start()
            outs.append(copy)
    for copy in outs:
        copy.wait()


def outbound_pages(ids, prefix, owners, mine, theirs, own, recv, devices):
    pages, rows, width = own.shape
    return pl.pallas_call(
        outbound_body,
        out_shape=jax.ShapeDtypeStruct((devices, rows + TAIL, width), BF16),
        grid_spec=pltpu.PrefetchScalarGridSpec(
            num_scalar_prefetch=2,
            grid=(1,),
            in_specs=[owner_block(owners), decay_block(mine), decay_block(theirs), IN_HBM, IN_HBM],
            out_specs=IN_HBM,
            scratch_shapes=[
                pltpu.VMEM(own.shape, BF16),
                pltpu.VMEM(own.shape, BF16),
                pltpu.VMEM((pages, rows + TAIL, width), BF16),
                pltpu.SemaphoreType.DMA((PARTS,)),
                pltpu.SemaphoreType.DMA((PARTS,)),
                pltpu.SemaphoreType.DMA((pages,)),
            ],
        ),
        compiler_params=pltpu.CompilerParams(vmem_limit_bytes=GRANT),
        cost_estimate=cost(pages * rows * width * 3, pages * rows * width * 6),
        name="outbound_pages",
    )(ids, prefix, owners, mine, theirs, own, recv)


def start_body(
    id_ref, prefix_ref, owner_ref, mine_ref, theirs_ref, in_ref, own_hbm, recv_hbm, start_hbm, send_hbm,
    page_ref, state_ref, held_ref, moved_ref, sem, state_sem, held_sem, moved_sem,
):
    pages = page_ref.shape[0]
    keep = jnp.where(prefix_ref[id_ref[0]] > 0, 1.0, 0.0)

    def run(decay_ref, state_hbm, held_hbm, moved_hbm):
        states = part_copies(state_hbm, state_ref, state_sem, PARTS)
        held_out = part_copies(held_ref, held_hbm, held_sem, PARTS)
        moved_out = part_copies(moved_ref, moved_hbm, moved_sem, PARTS)
        fetches = []
        for page in range(pages):
            owner = owner_of(owner_ref, id_ref, page, pages)
            fetches.append(pltpu.make_async_copy(in_ref.at[owner], page_ref.at[page], sem.at[page]))
        for c in range(PARTS):
            states[c].start()
            for k in range(pages // PARTS):
                fetches[c * (pages // PARTS) + k].start()
        for c in range(PARTS):
            states[c].wait()
            for k in range(pages // PARTS):
                fetches[c * (pages // PARTS) + k].wait()
            for k in range(pages // PARTS):
                page = c * (pages // PARTS) + k
                held = page_ref[page].astype(F32) * keep
                decay = decay_ref[0, id_ref[1] * pages + page]
                held_ref[page] = held.astype(BF16)
                moved_ref[page] = (decay * held + state_ref[page].astype(F32)).astype(BF16)
            held_out[c].start()
            moved_out[c].start()
        for copy in held_out + moved_out:
            copy.wait()

    @pl.when(id_ref[1] == 0)
    def _():
        run(mine_ref, own_hbm, start_hbm, send_hbm)

    @pl.when(id_ref[1] != 0)
    def _():
        run(theirs_ref, recv_hbm, send_hbm, start_hbm)


def start_states(ids, prefix, owners, mine, theirs, incoming, own, recv):
    pages, rows, width = own.shape
    return pl.pallas_call(
        start_body,
        out_shape=(jax.ShapeDtypeStruct(own.shape, BF16),) * 2,
        grid_spec=pltpu.PrefetchScalarGridSpec(
            num_scalar_prefetch=2,
            grid=(1,),
            in_specs=[owner_block(owners), decay_block(mine), decay_block(theirs)] + [IN_HBM] * 3,
            out_specs=[IN_HBM, IN_HBM],
            scratch_shapes=[pltpu.VMEM(own.shape, BF16)] * 4
            + [pltpu.SemaphoreType.DMA((pages,))]
            + [pltpu.SemaphoreType.DMA((PARTS,))] * 3,
        ),
        compiler_params=pltpu.CompilerParams(vmem_limit_bytes=GRANT),
        cost_estimate=cost(pages * rows * width * 4, pages * rows * width * 8),
        name="start_states",
    )(ids, prefix, owners, mine, theirs, incoming, own, recv)


def mixer_body(
    own, id_ref, count_ref, skip_ref, x_ref, bc_ref, cum_ref, shift_ref, start_ref, gate_ref,
    norm_ref, *rest
):
    out_ref, cols_ref, score_ref, gated_ref = rest[-4:]
    group = first_group(id_ref, own) + pl.program_id(0)
    rows, width = x_ref.shape
    pairs = width // LANES
    half = rows // 2
    first = lax.broadcasted_iota(jnp.int32, (rows, LANES), 1) < LANES // 2
    cols_ref[...] = group_heads(cum_ref, group, 2 * pairs)
    nstate = start_ref.shape[1]
    b_val, c_val = bc_ref[:, :nstate], bc_ref[:, nstate:]
    nt = (((1,), (1,)), ((), ()))
    scores = lax.dot_general(c_val, b_val, nt, preferred_element_type=F32)
    lower = (
        lax.broadcasted_iota(jnp.int32, (rows, rows), 0)
        >= lax.broadcasted_iota(jnp.int32, (rows, rows), 1)
    )
    score_ref[...] = jnp.where(lower, scores, 0.0)
    squares = jnp.zeros((rows, LANES), F32)
    for p in range(pairs):
        lanes = slice(p * LANES, (p + 1) * LANES)
        x_val = x_ref[:, lanes]
        left, right, both = pair_columns(cols_ref, p, first)
        ys = []
        for cum, h in ((left, 2 * p), (right, 2 * p + 1)):
            early = shift_ref[h : h + 1, :half]
            late = shift_ref[h : h + 1, half:]
            w00 = score_ref[:half, :half] * jnp.exp(jnp.minimum(cum[:half] - early, TOP))
            w10 = score_ref[half:, :half] * jnp.exp(cum[half:] - early)
            w11 = score_ref[half:, half:] * jnp.exp(jnp.minimum(cum[half:] - late, TOP))
            y0 = jnp.dot(w00.astype(BF16), x_val[:half], preferred_element_type=F32)
            w1 = jnp.concatenate([w10.astype(BF16), w11.astype(BF16)], axis=1)
            y1 = jnp.dot(w1, x_val, preferred_element_type=F32)
            ys.append(jnp.concatenate([y0, y1], axis=0))
        carried = lax.dot_general(c_val, start_ref[lanes, :], nt, preferred_element_type=F32)
        y = jnp.where(first, ys[0], ys[1]) + jnp.exp(both) * carried
        head = group * 2 * pairs + 2 * p
        skip = jnp.where(first, skip_ref[head], skip_ref[head + 1])
        y = y + skip * x_val.astype(F32)
        gated = y * silu(gate_ref[0, :, lanes].astype(F32))
        gated_ref[p] = gated
        squares = squares + gated * gated
    mean = jnp.sum(squares, axis=1, keepdims=True) * (1.0 / width)
    pos = id_ref[1] * rows + lax.broadcasted_iota(jnp.int32, (rows, 1), 0)
    live = pos < count_ref[id_ref[0]]
    factor = jnp.where(live, lax.rsqrt(mean + 1e-05), 0.0)
    factor = jnp.broadcast_to(factor, (rows, LANES))
    for p in range(pairs):
        lanes = slice(p * LANES, (p + 1) * LANES)
        at = pl.ds(pl.multiple_of(group * width + p * LANES, LANES), LANES)
        out_ref[0, :, lanes] = (gated_ref[p] * factor * norm_ref[:, at]).astype(BF16)


def mixer_half(own, ids, counts, skip, x, bc, cum, shift, start, gate, norm, so_far):
    rows, half_width = x.shape
    heads = cum.shape[1]
    half = GROUPS // 2
    width = half_width // half
    nstate = start.shape[1]
    per_group = heads // GROUPS
    in_specs = [
        pl.BlockSpec((rows, width), lambda i, a, *s: (0, i)),
        pl.BlockSpec((rows, 2 * nstate), lambda i, a, *s: (0, i)),
        pl.BlockSpec((rows, heads), lambda i, a, *s: (0, 0)),
        pl.BlockSpec((per_group, rows), lambda i, a, *s: (first_group(a, own) + i, 0)),
        pl.BlockSpec((width, nstate), lambda i, a, *s: (i, 0)),
        pl.BlockSpec((1, rows, width), lambda i, a, *s: (0, 0, first_group(a, own) + i)),
        pl.BlockSpec(norm.shape, lambda i, a, *s: (0, 0)),
    ]
    args = [ids, counts, skip, x, bc, cum, shift, start, gate, norm]
    aliases = {}
    if so_far is not None:
        in_specs.append(pl.BlockSpec(memory_space=pl.ANY))
        aliases = {len(args): 0}
        args.append(so_far)
    return pl.pallas_call(
        functools.partial(mixer_body, own),
        out_shape=jax.ShapeDtypeStruct(gate.shape, BF16),
        grid_spec=pltpu.PrefetchScalarGridSpec(
            num_scalar_prefetch=3,
            grid=(half,),
            in_specs=in_specs,
            out_specs=pl.BlockSpec((1, rows, width), lambda i, a, *s: (0, 0, first_group(a, own) + i)),
            scratch_shapes=[
                pltpu.VMEM((rows, heads), F32),
                pltpu.VMEM((rows, rows), F32),
                pltpu.VMEM((width // LANES, rows, LANES), F32),
            ],
        ),
        input_output_aliases=aliases,
        compiler_params=pltpu.CompilerParams(vmem_limit_bytes=GRANT),
        cost_estimate=cost(
            rows * half_width * (2 * rows + 2 * nstate), rows * half_width * 8, rows * rows * heads // 2
        ),
        name="mixer_half",
    )(*args)


def pool_body(dev_ref, pool_hbm, in_hbm, out_hbm, in_ref, pool_ref, new_ref, in_sem, pool_sem, out_sem):
    slots, rows, _ = pool_ref.shape
    parts = 2 * PARTS
    size = slots // parts
    pages = part_copies(in_hbm, in_ref, in_sem, PARTS)
    pools = part_copies(pool_hbm, pool_ref, pool_sem, parts)
    outs = part_copies(new_ref, out_hbm, out_sem, parts)
    for copy in pages + pools:
        copy.start()
    for copy in pages:
        copy.wait()
    for c in range(parts):
        pools[c].wait()
        for k in range(size):
            slot = c * size + k
            device = dev_ref[slot]
            at = jnp.maximum(device, 0)
            tail = in_ref[at, rows:].astype(F32)
            whole = tail[0:1] + tail[1:2]
            old = pool_ref[slot]
            new = whole * old + in_ref[at, :rows].astype(F32)
            new_ref[slot] = jnp.where(device >= 0, new, old)
        outs[c].start()
    for copy in outs:
        copy.wait()


def updated_pool(dev_of_slot, pool, returned):
    slots, rows, width = pool.shape
    return pl.pallas_call(
        pool_body,
        out_shape=jax.ShapeDtypeStruct(pool.shape, F32),
        grid_spec=pltpu.PrefetchScalarGridSpec(
            num_scalar_prefetch=1,
            grid=(1,),
            in_specs=[IN_HBM, IN_HBM],
            out_specs=IN_HBM,
            scratch_shapes=[
                pltpu.VMEM(returned.shape, BF16),
                pltpu.VMEM(pool.shape, F32),
                pltpu.VMEM(pool.shape, F32),
                pltpu.SemaphoreType.DMA((PARTS,)),
                pltpu.SemaphoreType.DMA((2 * PARTS,)),
                pltpu.SemaphoreType.DMA((2 * PARTS,)),
            ],
        ),
        compiler_params=pltpu.CompilerParams(vmem_limit_bytes=GRANT),
        cost_estimate=cost(slots * rows * width * 2, slots * rows * width * 10),
        name="updated_pool",
    )(dev_of_slot, pool, returned)


def local(
    conv_input,
    gate_input,
    dt_raw,
    conv_weight,
    conv_bias,
    dt_bias,
    a_log,
    d_skip,
    norm_weight,
    conv_cache,
    state_pool,
    page_owner,
    page_slot,
    prefix_len,
    new_count,
):
    ctx_count = lax.axis_size("ctx")
    devices = lax.axis_size("req") * ctx_count
    req_index = lax.axis_index("req")
    ctx_index = lax.axis_index("ctx")
    own_index = req_index * ctx_count + ctx_index
    rows = conv_input.shape[1]
    heads = dt_raw.shape[2]
    inner = gate_input.shape[2]
    slots, page_rows, nstate = state_pool.shape
    pages = page_owner.shape[1] // ctx_count
    rim = conv_weight.shape[0] - 1
    requests = page_owner.shape[0]

    matches = page_owner == own_index
    early = jnp.arange(2 * pages)[None, :] < pages
    slot_0 = jnp.max(jnp.where(matches & early, page_slot, -1), axis=1)
    slot_1 = jnp.max(jnp.where(matches & ~early, page_slot, -1), axis=1)
    outgoing = gather_pages(slot_0, slot_1, state_pool, devices)
    outgoing, conv_input, dt_raw, new_count, prefix_len, page_owner = lax.optimization_barrier(
        (outgoing, conv_input, dt_raw, new_count, prefix_len, page_owner)
    )
    incoming = lax.all_to_all(outgoing, ("req", "ctx"), split_axis=0, concat_axis=0, tiled=True)

    ids = jnp.stack([req_index, ctx_index]).astype(jnp.int32)
    previous = lax.ppermute(conv_input[0, rows - rim :], "ctx", [(0, 1)])
    cum, shift, ending, decay_rows = step_tables(ids, new_count, dt_raw, dt_bias, a_log)
    other_decay = swapped(decay_rows)

    conv_args = (
        conv_input, conv_cache, previous, conv_weight, conv_bias[None], ending, inner, nstate
    )
    x_other, bc_other, state_other, tail = conv_half(False, ids, prefix_len, new_count, None, *conv_args)
    received = swapped(state_other)
    x_own, bc_own, state_own, tail = conv_half(True, ids, prefix_len, new_count, tail, *conv_args)
    as_pages = lambda value: value.reshape(pages, page_rows, nstate)
    own_pages, recv_pages = as_pages(state_own), as_pages(received)
    page_args = (ids, prefix_len, page_owner, decay_rows, other_decay)
    outbound = outbound_pages(*page_args, own_pages, recv_pages, devices)
    returned = lax.all_to_all(outbound, ("req", "ctx"), split_axis=0, concat_axis=0, tiled=True)

    start, send = start_states(*page_args, incoming, own_pages, recv_pages)
    start, slot_0, slot_1, late_count, tail = lax.optimization_barrier(
        (start, slot_0, slot_1, new_count, tail)
    )
    start_other = swapped(send)
    as_rows = lambda value: value.reshape(pages * page_rows, nstate)
    mixed = mixer_half(
        True, ids, new_count, d_skip, x_own, bc_own, cum, shift, as_rows(start), gate_input,
        norm_weight[None], None,
    )
    mixed = mixer_half(
        False, ids, new_count, d_skip, x_other, bc_other, cum, shift, as_rows(start_other),
        gate_input, norm_weight[None], mixed,
    )

    other_tail = swapped(tail)
    mine = (late_count[req_index] > rows) == (ctx_index == 1)
    new_tail = jnp.where(mine, tail, other_tail)[:rim]
    slot_ids = jnp.arange(slots, dtype=jnp.int32)[:, None]
    request_ids = jnp.arange(requests, dtype=jnp.int32)[None, :]
    hits_0, hits_1 = slot_0[None, :] == slot_ids, slot_1[None, :] == slot_ids
    dev_of_slot = jnp.max(
        jnp.maximum(
            jnp.where(hits_0, 2 * request_ids, -1), jnp.where(hits_1, 2 * request_ids + 1, -1)
        ),
        axis=1,
    )
    new_pool = updated_pool(dev_of_slot, state_pool, returned)
    return (mixed, new_tail[None], new_pool)


def solution(mesh):
    return jax.shard_map(
        local,
        mesh=mesh,
        in_specs=(
            P("req", "ctx", None),
            P("req", "ctx", None),
            P("req", "ctx", None),
            P(),
            P(),
            P(),
            P(),
            P(),
            P(),
            P("req", None, None),
            P(("req", "ctx"), None, None),
            P(),
            P(),
            P(),
            P(),
        ),
        out_specs=(P("req", "ctx", None), P("req", None, None), P(("req", "ctx"), None, None)),
        check_vma=False,
    )
```

```python
import functools

import jax
import jax.numpy as jnp
from jax import lax
from jax.experimental import pallas as pl
from jax.experimental.pallas import tpu as pltpu
from jax.sharding import PartitionSpec as P

GROUPS = 8
LANES = 128
TAIL = 8
PARTS = 4
GRANT = 64 << 20
TOP = 88.72
F32 = jnp.float32
IN_HBM = pl.BlockSpec(memory_space=pltpu.HBM)
BF16 = jnp.bfloat16


def swapped(value):
    return lax.ppermute(value, "ctx", [(0, 1), (1, 0)])


def silu(value):
    half = 0.5 * value
    return half + half * jnp.tanh(half)


def cost(flops, nbytes, trans=0):
    return pl.CostEstimate(flops=flops, bytes_accessed=nbytes, transcendentals=trans)


def part_copies(source, target, sems, parts):
    size = source.shape[0] // parts
    return [
        pltpu.make_async_copy(
            source.at[pl.ds(c * size, size)], target.at[pl.ds(c * size, size)], sems.at[c]
        )
        for c in range(parts)
    ]


def gather_body(
    early_ref, late_ref, pool_ref, tokens_ref, out_ref, last_ref, page_ref, round_ref, deep_ref,
    in_sem, out_sem, deep_sem,
):
    devices = round_ref.shape[0]
    deep = deep_ref.shape[0]
    rim = last_ref.shape[0]
    ins = part_copies(pool_ref, page_ref, in_sem, PARTS)
    outs = part_copies(round_ref, out_ref, out_sem, PARTS)
    rows = pltpu.make_async_copy(
        tokens_ref.at[0, pl.ds(tokens_ref.shape[1] - deep, deep)], deep_ref, deep_sem
    )
    rows.start()
    for copy in ins:
        copy.start()
    rows.wait()
    last_ref[...] = deep_ref[...].astype(F32)[deep - rim :].astype(BF16)
    for copy in ins:
        copy.wait()
    for c in range(PARTS):
        for k in range(devices // PARTS):
            device = c * (devices // PARTS) + k
            slot = (early_ref, late_ref)[device % 2][device // 2]
            round_ref[device] = page_ref[jnp.maximum(slot, 0)].astype(BF16)
        outs[c].start()
    for copy in outs:
        copy.wait()


def gather_pages(slot_early, slot_late, pool, tokens, devices, rim):
    slots, rows, width = pool.shape
    channels = tokens.shape[2]
    return pl.pallas_call(
        gather_body,
        out_shape=(
            jax.ShapeDtypeStruct((devices, rows, width), BF16),
            jax.ShapeDtypeStruct((rim, channels), BF16),
        ),
        grid_spec=pltpu.PrefetchScalarGridSpec(
            num_scalar_prefetch=2,
            grid=(1,),
            in_specs=[IN_HBM, IN_HBM],
            out_specs=[IN_HBM, pl.BlockSpec((rim, channels), lambda i, *s: (0, 0))],
            scratch_shapes=[
                pltpu.VMEM((slots, rows, width), F32),
                pltpu.VMEM((devices, rows, width), BF16),
                pltpu.VMEM((16, channels), BF16),
                pltpu.SemaphoreType.DMA((PARTS,)),
                pltpu.SemaphoreType.DMA((PARTS,)),
                pltpu.SemaphoreType.DMA,
            ],
        ),
        compiler_params=pltpu.CompilerParams(vmem_limit_bytes=GRANT),
        cost_estimate=cost(slots * rows * width, slots * rows * width * 6),
        name="gather_pages",
    )(slot_early, slot_late, pool, tokens)


def steps_body(id_ref, count_ref, raw_ref, bias_ref, alog_ref, cum_ref, shift_ref, ending_ref, decay_ref):
    rows, heads = cum_ref.shape
    pos = id_ref[1] * rows + lax.broadcasted_iota(jnp.int32, (rows, heads), 0)
    live = pos < count_ref[id_ref[0]]
    value = raw_ref[0].astype(F32) + bias_ref[...]
    soft = jnp.maximum(value, 0.0) + jnp.log1p(jnp.exp(-jnp.abs(value)))
    dt = jnp.where(live, soft, 0.0)
    la = -jnp.exp(alog_ref[...]) * dt
    tri = (
        lax.broadcasted_iota(jnp.int32, (rows, rows), 0)
        >= lax.broadcasted_iota(jnp.int32, (rows, rows), 1)
    )
    tri = jnp.where(tri, 1.0, 0.0).astype(BF16)
    high = la.astype(BF16)
    rest = la - high.astype(F32)
    mid = rest.astype(BF16)
    low = (rest - mid.astype(F32)).astype(BF16)
    cum = (
        jnp.dot(tri, low, preferred_element_type=F32)
        + jnp.dot(tri, mid, preferred_element_type=F32)
        + jnp.dot(tri, high, preferred_element_type=F32)
    )
    last = cum[rows - 1 :, :]
    cum_ref[...] = cum
    some = dt > 0.0
    log_dt = jnp.where(some, jnp.log(jnp.where(some, dt, 1.0)), -1e30)
    shift_ref[...] = (cum - log_dt).T
    ending_ref[...] = jnp.exp(last - cum) * dt
    decay_ref[...] = jnp.broadcast_to(jnp.exp(last), decay_ref.shape)


def step_tables(ids, counts, dt_raw, dt_bias, a_log):
    _, rows, heads = dt_raw.shape
    whole = lambda *shape: pl.BlockSpec(shape, lambda i, *s: (0,) * len(shape))
    return pl.pallas_call(
        steps_body,
        out_shape=(
            jax.ShapeDtypeStruct((rows, heads), F32),
            jax.ShapeDtypeStruct((heads, rows), F32),
            jax.ShapeDtypeStruct((rows, heads), F32),
            jax.ShapeDtypeStruct((8, heads), F32),
        ),
        grid_spec=pltpu.PrefetchScalarGridSpec(
            num_scalar_prefetch=2,
            grid=(1,),
            in_specs=[whole(1, rows, heads), whole(1, heads), whole(1, heads)],
            out_specs=[whole(rows, heads), whole(heads, rows), whole(rows, heads), whole(8, heads)],
        ),
        compiler_params=pltpu.CompilerParams(vmem_limit_bytes=GRANT),
        cost_estimate=cost(rows * rows * heads * 6, rows * heads * 16, rows * heads * 4),
        name="step_tables",
    )(ids, counts, dt_raw, dt_bias[None], a_log[None])


def pair_columns(table, p, first):
    rows = table.shape[0]
    left = jnp.broadcast_to(table[:, 2 * p : 2 * p + 1], (rows, LANES))
    right = jnp.broadcast_to(table[:, 2 * p + 1 : 2 * p + 2], (rows, LANES))
    return left, right, jnp.where(first, left, right)


def first_group(id_ref, own):
    ctx = id_ref[1]
    return (ctx if own else 1 - ctx) * (GROUPS // 2)


def group_heads(ref, group, per_group):
    heads = ref.shape[1]
    return pltpu.roll(ref[...], lax.rem(heads - group * per_group, heads), 1)


def conv_body(
    own, channels, id_ref, prefix_ref, count_ref, x_ref, b_ref, c_ref, cache_ref, before_ref, weight_ref, bias_ref,
    ending_ref, *rest
):
    xa_ref, bc_ref, state_ref, tail_ref, rows_ref, cols_ref = rest[-6:]
    group = first_group(id_ref, own) + pl.program_id(0)
    rows = x_ref.shape[1]
    width = x_ref.shape[2]
    nstate = b_ref.shape[2]
    pairs = width // LANES
    taps = weight_ref.shape[0]
    b_at, c_at = channels
    first = lax.broadcasted_iota(jnp.int32, (rows, LANES), 1) < LANES // 2
    cols_ref[...] = group_heads(ending_ref, group, 2 * pairs)
    held = lax.broadcasted_iota(jnp.int32, (taps - 1, LANES), 0) >= taps - 1 - prefix_ref[id_ref[0]]
    lead = id_ref[1] == 0
    last = count_ref[id_ref[0]] - id_ref[1] * rows
    newest = 9 - taps + jnp.clip(last, 0, rows)
    here = (count_ref[id_ref[0]] > rows) == (id_ref[1] == 1)
    if own:

        @pl.when(pl.program_id(0) == 0)
        def _():
            tail_ref[...] = rest[0][...]

    def conv(slot, src, at, begin):
        lanes = pl.ds(pl.multiple_of(begin, LANES), LANES)
        cached = jnp.where(held, cache_ref[0, :, lanes].astype(F32), 0.0)
        rim = jnp.where(lead, cached, before_ref[:, lanes].astype(F32))
        rows_ref[slot, 9 - taps : 8] = rim
        rows_ref[slot, 8 : 8 + rows] = src[0, :, at : at + LANES].astype(F32)
        tail_ref[:, lanes] = jnp.where(here, rows_ref[slot, pl.ds(newest, 8)], 0.0).astype(BF16)
        total = bias_ref[:, lanes]
        weight = weight_ref[:, lanes]
        for k in range(taps):
            start = 9 - taps + k
            total = total + weight[k : k + 1] * rows_ref[slot, start : start + rows]
        return silu(total).astype(BF16)

    bc_ref[:, :nstate] = conv(0, b_ref, 0, b_at + group * nstate)
    bc_ref[:, nstate:] = conv(1, c_ref, 0, c_at + group * nstate)
    b_turned = bc_ref[:, :nstate].T
    nt = (((1,), (1,)), ((), ()))
    down = lax.broadcasted_iota(jnp.int32, (LANES, LANES), 0)
    across = lax.broadcasted_iota(jnp.int32, (LANES, LANES), 1)
    same = jnp.where(down == across, 1.0, 0.0).astype(BF16)
    for p in range(pairs):
        act = conv(p % 2, x_ref, p * LANES, group * width + p * LANES)
        xa_ref[:, p * LANES : (p + 1) * LANES] = act
        _, _, ending = pair_columns(cols_ref, p, first)
        scaled = (act.astype(F32) * ending).astype(BF16)
        turned = jnp.dot(b_turned, scaled, preferred_element_type=F32).astype(BF16)
        state = lax.dot_general(same, turned, nt, preferred_element_type=F32)
        state_ref[p * LANES : (p + 1) * LANES, :] = state.astype(BF16)


def conv_half(own, ids, prefix, counts, tail, tokens, cache, before, weight, bias, ending, inner, nstate):
    _, rows, channels = tokens.shape
    heads = ending.shape[1]
    width = inner // GROUPS
    half = GROUPS // 2
    b_at, c_at = inner, inner + GROUPS * nstate

    def channel_block(wide, begin):
        return pl.BlockSpec(
            (1, rows, wide), lambda i, a, *s: (0, 0, begin // wide + first_group(a, own) + i)
        )

    def whole(value):
        return pl.BlockSpec(value.shape, lambda i, *s: (0,) * value.ndim)

    tails = [] if tail is None else [tail]
    return pl.pallas_call(
        functools.partial(conv_body, own, (b_at, c_at)),
        out_shape=(
            jax.ShapeDtypeStruct((rows, half * width), BF16),
            jax.ShapeDtypeStruct((rows, half * 2 * nstate), BF16),
            jax.ShapeDtypeStruct((half * width, nstate), BF16),
            jax.ShapeDtypeStruct((8, channels), BF16),
        ),
        grid_spec=pltpu.PrefetchScalarGridSpec(
            num_scalar_prefetch=3,
            grid=(half,),
            in_specs=[
                channel_block(width, 0),
                channel_block(nstate, b_at),
                channel_block(nstate, c_at),
                whole(cache),
                whole(before),
                whole(weight),
                whole(bias),
                whole(ending),
            ]
            + [whole(value) for value in tails],
            out_specs=[
                pl.BlockSpec((rows, width), lambda i, *s: (0, i)),
                pl.BlockSpec((rows, 2 * nstate), lambda i, *s: (0, i)),
                pl.BlockSpec((width, nstate), lambda i, *s: (i, 0)),
                pl.BlockSpec((8, channels), lambda i, *s: (0, 0)),
            ],
            scratch_shapes=[pltpu.VMEM((2, rows + 16, LANES), F32), pltpu.VMEM((rows, heads), F32)],
        ),
        compiler_params=pltpu.CompilerParams(vmem_limit_bytes=GRANT),
        cost_estimate=cost(rows * channels * 40, rows * channels * 2, rows * channels // 2),
        name="conv_half",
    )(ids, prefix, counts, tokens, tokens, tokens, cache, before, weight, bias, ending, *tails)


def owner_of(owner_ref, id_ref, page, pages):
    return owner_ref[lax.rem(id_ref[0], owner_ref.shape[0]), id_ref[1] * pages + page]


def owner_block(owners):
    deep = min(8, owners.shape[0])
    return pl.BlockSpec(
        (deep, owners.shape[1]), lambda i, d, *s: (d[0] // deep, 0), memory_space=pltpu.SMEM
    )


def decay_block(decay):
    return pl.BlockSpec(decay.shape, lambda i, *s: (0, 0), memory_space=pltpu.SMEM)


def outbound_body(id_ref, prefix_ref, owner_ref, mine_ref, theirs_ref, own_ref, recv_ref, out_ref):
    chunk, rows, width = own_ref.shape
    pages = chunk * pl.num_programs(0)
    lead = id_ref[1] == 0
    keep = jnp.where(prefix_ref[id_ref[0]] > 0, 1.0, 0.0)
    top = lax.broadcasted_iota(jnp.int32, (TAIL, width), 0) == 0
    for k in range(chunk):
        page = pl.program_id(0) * chunk + k
        head = id_ref[1] * pages + page
        mine, theirs = mine_ref[0, head], theirs_ref[0, head]
        own_w = jnp.where(lead, theirs, 1.0)
        recv_w = jnp.where(lead, 1.0, mine)
        total = own_w * own_ref[k].astype(F32) + recv_w * recv_ref[k].astype(F32)
        whole = jnp.full((TAIL, width), mine * theirs * keep, F32)
        high = whole.astype(BF16).astype(F32)
        owner = owner_of(owner_ref, id_ref, page, pages)
        out_ref[owner, :rows] = total.astype(BF16)
        out_ref[owner, rows:] = jnp.where(top, high, whole - high).astype(BF16)


def outbound_pages(ids, prefix, owners, mine, theirs, own, recv, devices):
    pages, rows, width = own.shape
    chunk = pages // 2
    return pl.pallas_call(
        outbound_body,
        out_shape=jax.ShapeDtypeStruct((devices, rows + TAIL, width), BF16),
        grid_spec=pltpu.PrefetchScalarGridSpec(
            num_scalar_prefetch=2,
            grid=(pages // chunk,),
            in_specs=[owner_block(owners), decay_block(mine), decay_block(theirs)]
            + [pl.BlockSpec((chunk, rows, width), lambda i, *s: (i, 0, 0))] * 2,
            out_specs=pl.BlockSpec((devices, rows + TAIL, width), lambda i, *s: (0, 0, 0)),
        ),
        compiler_params=pltpu.CompilerParams(vmem_limit_bytes=GRANT),
        cost_estimate=cost(pages * rows * width * 3, pages * rows * width * 8),
        name="outbound_pages",
    )(ids, prefix, owners, mine, theirs, own, recv)


def start_body(
    id_ref, prefix_ref, owner_ref, mine_ref, theirs_ref, in_ref, own_hbm, recv_hbm, start_hbm, send_hbm,
    page_ref, state_ref, held_ref, moved_ref, sem, state_sem, held_sem, moved_sem,
):
    pages = page_ref.shape[0]
    keep = jnp.where(prefix_ref[id_ref[0]] > 0, 1.0, 0.0)

    def run(decay_ref, state_hbm, held_hbm, moved_hbm):
        states = part_copies(state_hbm, state_ref, state_sem, PARTS)
        held_out = part_copies(held_ref, held_hbm, held_sem, PARTS)
        moved_out = part_copies(moved_ref, moved_hbm, moved_sem, PARTS)
        fetches = []
        for page in range(pages):
            owner = owner_of(owner_ref, id_ref, page, pages)
            fetches.append(pltpu.make_async_copy(in_ref.at[owner], page_ref.at[page], sem.at[page]))
        for c in range(PARTS):
            states[c].start()
            for k in range(pages // PARTS):
                fetches[c * (pages // PARTS) + k].start()
        for c in range(PARTS):
            states[c].wait()
            for k in range(pages // PARTS):
                fetches[c * (pages // PARTS) + k].wait()
            for k in range(pages // PARTS):
                page = c * (pages // PARTS) + k
                held = page_ref[page].astype(F32) * keep
                decay = decay_ref[0, id_ref[1] * pages + page]
                held_ref[page] = held.astype(BF16)
                moved_ref[page] = (decay * held + state_ref[page].astype(F32)).astype(BF16)
            held_out[c].start()
            moved_out[c].start()
        for copy in held_out + moved_out:
            copy.wait()

    @pl.when(id_ref[1] == 0)
    def _():
        run(mine_ref, own_hbm, start_hbm, send_hbm)

    @pl.when(id_ref[1] != 0)
    def _():
        run(theirs_ref, recv_hbm, send_hbm, start_hbm)


def start_states(ids, prefix, owners, mine, theirs, incoming, own, recv):
    pages, rows, width = own.shape
    return pl.pallas_call(
        start_body,
        out_shape=(jax.ShapeDtypeStruct(own.shape, BF16),) * 2,
        grid_spec=pltpu.PrefetchScalarGridSpec(
            num_scalar_prefetch=2,
            grid=(1,),
            in_specs=[owner_block(owners), decay_block(mine), decay_block(theirs)] + [IN_HBM] * 3,
            out_specs=[IN_HBM, IN_HBM],
            scratch_shapes=[pltpu.VMEM(own.shape, BF16)] * 4
            + [pltpu.SemaphoreType.DMA((pages,))]
            + [pltpu.SemaphoreType.DMA((PARTS,))] * 3,
        ),
        compiler_params=pltpu.CompilerParams(vmem_limit_bytes=GRANT),
        cost_estimate=cost(pages * rows * width * 4, pages * rows * width * 8),
        name="start_states",
    )(ids, prefix, owners, mine, theirs, incoming, own, recv)


def mixer_body(
    own, id_ref, count_ref, skip_ref, x_ref, bc_ref, cum_ref, shift_ref, start_ref, gate_ref,
    norm_ref, *rest
):
    out_ref, cols_ref, score_ref, gated_ref = rest[-4:]
    group = first_group(id_ref, own) + pl.program_id(0)
    rows, width = x_ref.shape
    pairs = width // LANES
    half = rows // 2
    first = lax.broadcasted_iota(jnp.int32, (rows, LANES), 1) < LANES // 2
    cols_ref[...] = group_heads(cum_ref, group, 2 * pairs)
    nstate = start_ref.shape[1]
    b_val, c_val = bc_ref[:, :nstate], bc_ref[:, nstate:]
    nt = (((1,), (1,)), ((), ()))
    scores = lax.dot_general(c_val, b_val, nt, preferred_element_type=F32)
    lower = (
        lax.broadcasted_iota(jnp.int32, (rows, rows), 0)
        >= lax.broadcasted_iota(jnp.int32, (rows, rows), 1)
    )
    score_ref[...] = jnp.where(lower, scores, 0.0)
    squares = jnp.zeros((rows, LANES), F32)
    for p in range(pairs):
        lanes = slice(p * LANES, (p + 1) * LANES)
        x_val = x_ref[:, lanes]
        left, right, both = pair_columns(cols_ref, p, first)
        ys = []
        for cum, h in ((left, 2 * p), (right, 2 * p + 1)):
            early = shift_ref[h : h + 1, :half]
            late = shift_ref[h : h + 1, half:]
            w00 = score_ref[:half, :half] * jnp.exp(jnp.minimum(cum[:half] - early, TOP))
            w10 = score_ref[half:, :half] * jnp.exp(cum[half:] - early)
            w11 = score_ref[half:, half:] * jnp.exp(jnp.minimum(cum[half:] - late, TOP))
            y0 = jnp.dot(w00.astype(BF16), x_val[:half], preferred_element_type=F32)
            w1 = jnp.concatenate([w10.astype(BF16), w11.astype(BF16)], axis=1)
            y1 = jnp.dot(w1, x_val, preferred_element_type=F32)
            ys.append(jnp.concatenate([y0, y1], axis=0))
        carried = lax.dot_general(c_val, start_ref[lanes, :], nt, preferred_element_type=F32)
        y = jnp.where(first, ys[0], ys[1]) + jnp.exp(both) * carried
        head = group * 2 * pairs + 2 * p
        skip = jnp.where(first, skip_ref[head], skip_ref[head + 1])
        y = y + skip * x_val.astype(F32)
        gated = y * silu(gate_ref[0, :, lanes].astype(F32))
        gated_ref[p] = gated
        squares = squares + gated * gated
    mean = jnp.sum(squares, axis=1, keepdims=True) * (1.0 / width)
    pos = id_ref[1] * rows + lax.broadcasted_iota(jnp.int32, (rows, 1), 0)
    live = pos < count_ref[id_ref[0]]
    factor = jnp.where(live, lax.rsqrt(mean + 1e-05), 0.0)
    factor = jnp.broadcast_to(factor, (rows, LANES))
    for p in range(pairs):
        lanes = slice(p * LANES, (p + 1) * LANES)
        at = pl.ds(pl.multiple_of(group * width + p * LANES, LANES), LANES)
        out_ref[0, :, lanes] = (gated_ref[p] * factor * norm_ref[:, at]).astype(BF16)


def mixer_half(own, ids, counts, skip, x, bc, cum, shift, start, gate, norm, so_far):
    rows, half_width = x.shape
    heads = cum.shape[1]
    half = GROUPS // 2
    width = half_width // half
    nstate = start.shape[1]
    per_group = heads // GROUPS
    in_specs = [
        pl.BlockSpec((rows, width), lambda i, a, *s: (0, i)),
        pl.BlockSpec((rows, 2 * nstate), lambda i, a, *s: (0, i)),
        pl.BlockSpec((rows, heads), lambda i, a, *s: (0, 0)),
        pl.BlockSpec((per_group, rows), lambda i, a, *s: (first_group(a, own) + i, 0)),
        pl.BlockSpec((width, nstate), lambda i, a, *s: (i, 0)),
        pl.BlockSpec((1, rows, width), lambda i, a, *s: (0, 0, first_group(a, own) + i)),
        pl.BlockSpec(norm.shape, lambda i, a, *s: (0, 0)),
    ]
    args = [ids, counts, skip, x, bc, cum, shift, start, gate, norm]
    aliases = {}
    if so_far is not None:
        in_specs.append(pl.BlockSpec(memory_space=pl.ANY))
        aliases = {len(args): 0}
        args.append(so_far)
    return pl.pallas_call(
        functools.partial(mixer_body, own),
        out_shape=jax.ShapeDtypeStruct(gate.shape, BF16),
        grid_spec=pltpu.PrefetchScalarGridSpec(
            num_scalar_prefetch=3,
            grid=(half,),
            in_specs=in_specs,
            out_specs=pl.BlockSpec((1, rows, width), lambda i, a, *s: (0, 0, first_group(a, own) + i)),
            scratch_shapes=[
                pltpu.VMEM((rows, heads), F32),
                pltpu.VMEM((rows, rows), F32),
                pltpu.VMEM((width // LANES, rows, LANES), F32),
            ],
        ),
        input_output_aliases=aliases,
        compiler_params=pltpu.CompilerParams(vmem_limit_bytes=GRANT),
        cost_estimate=cost(
            rows * half_width * (2 * rows + 2 * nstate), rows * half_width * 8, rows * rows * heads // 2
        ),
        name="mixer_half",
    )(*args)


def pool_body(dev_ref, pool_hbm, in_hbm, out_hbm, in_ref, pool_ref, new_ref, in_sem, pool_sem, out_sem):
    slots, rows, _ = pool_ref.shape
    parts = 2 * PARTS
    size = slots // parts
    pages = part_copies(in_hbm, in_ref, in_sem, PARTS)
    pools = part_copies(pool_hbm, pool_ref, pool_sem, parts)
    outs = part_copies(new_ref, out_hbm, out_sem, parts)
    for copy in pages + pools:
        copy.start()
    for copy in pages:
        copy.wait()
    for c in range(parts):
        pools[c].wait()
        for k in range(size):
            slot = c * size + k
            device = dev_ref[slot]
            at = jnp.maximum(device, 0)
            tail = in_ref[at, rows:].astype(F32)
            whole = tail[0:1] + tail[1:2]
            old = pool_ref[slot]
            new = whole * old + in_ref[at, :rows].astype(F32)
            new_ref[slot] = jnp.where(device >= 0, new, old)
        outs[c].start()
    for copy in outs:
        copy.wait()


def updated_pool(dev_of_slot, pool, returned):
    slots, rows, width = pool.shape
    return pl.pallas_call(
        pool_body,
        out_shape=jax.ShapeDtypeStruct(pool.shape, F32),
        grid_spec=pltpu.PrefetchScalarGridSpec(
            num_scalar_prefetch=1,
            grid=(1,),
            in_specs=[IN_HBM, IN_HBM],
            out_specs=IN_HBM,
            scratch_shapes=[
                pltpu.VMEM(returned.shape, BF16),
                pltpu.VMEM(pool.shape, F32),
                pltpu.VMEM(pool.shape, F32),
                pltpu.SemaphoreType.DMA((PARTS,)),
                pltpu.SemaphoreType.DMA((2 * PARTS,)),
                pltpu.SemaphoreType.DMA((2 * PARTS,)),
            ],
        ),
        compiler_params=pltpu.CompilerParams(vmem_limit_bytes=GRANT),
        cost_estimate=cost(slots * rows * width * 2, slots * rows * width * 10),
        name="updated_pool",
    )(dev_of_slot, pool, returned)


def local(
    conv_input,
    gate_input,
    dt_raw,
    conv_weight,
    conv_bias,
    dt_bias,
    a_log,
    d_skip,
    norm_weight,
    conv_cache,
    state_pool,
    page_owner,
    page_slot,
    prefix_len,
    new_count,
):
    ctx_count = lax.axis_size("ctx")
    devices = lax.axis_size("req") * ctx_count
    req_index = lax.axis_index("req")
    ctx_index = lax.axis_index("ctx")
    own_index = req_index * ctx_count + ctx_index
    rows = conv_input.shape[1]
    heads = dt_raw.shape[2]
    inner = gate_input.shape[2]
    slots, page_rows, nstate = state_pool.shape
    pages = page_owner.shape[1] // ctx_count
    rim = conv_weight.shape[0] - 1
    requests = page_owner.shape[0]

    matches = page_owner == own_index
    early = jnp.arange(2 * pages)[None, :] < pages
    slot_0 = jnp.max(jnp.where(matches & early, page_slot, -1), axis=1)
    slot_1 = jnp.max(jnp.where(matches & ~early, page_slot, -1), axis=1)
    outgoing, last_rows = gather_pages(slot_0, slot_1, state_pool, conv_input, devices, rim)
    outgoing, conv_input, dt_raw, new_count, prefix_len, page_owner = lax.optimization_barrier(
        (outgoing, conv_input, dt_raw, new_count, prefix_len, page_owner)
    )
    incoming = lax.all_to_all(outgoing, ("req", "ctx"), split_axis=0, concat_axis=0, tiled=True)

    ids = jnp.stack([req_index, ctx_index]).astype(jnp.int32)
    previous = lax.ppermute(last_rows, "ctx", [(0, 1)])
    cum, shift, ending, decay_rows = step_tables(ids, new_count, dt_raw, dt_bias, a_log)
    other_decay = swapped(decay_rows)

    conv_args = (
        conv_input, conv_cache, previous, conv_weight, conv_bias[None], ending, inner, nstate
    )
    x_other, bc_other, state_other, tail = conv_half(False, ids, prefix_len, new_count, None, *conv_args)
    received = swapped(state_other)
    x_own, bc_own, state_own, tail = conv_half(True, ids, prefix_len, new_count, tail, *conv_args)
    as_pages = lambda value: value.reshape(pages, page_rows, nstate)
    own_pages, recv_pages = as_pages(state_own), as_pages(received)
    page_args = (ids, prefix_len, page_owner, decay_rows, other_decay)
    outbound = outbound_pages(*page_args, own_pages, recv_pages, devices)
    returned = lax.all_to_all(outbound, ("req", "ctx"), split_axis=0, concat_axis=0, tiled=True)

    start, send = start_states(*page_args, incoming, own_pages, recv_pages)
    start, slot_0, slot_1, tail = lax.optimization_barrier(
        (start, slot_0, slot_1, tail)
    )
    start_other = swapped(send)
    as_rows = lambda value: value.reshape(pages * page_rows, nstate)
    mixed = mixer_half(
        True, ids, new_count, d_skip, x_own, bc_own, cum, shift, as_rows(start), gate_input,
        norm_weight[None], None,
    )
    mixed = mixer_half(
        False, ids, new_count, d_skip, x_other, bc_other, cum, shift, as_rows(start_other),
        gate_input, norm_weight[None], mixed,
    )

    new_tail = (tail + swapped(tail))[:rim]
    slot_ids = lax.broadcasted_iota(jnp.int32, (slots, requests), 0)
    request_ids = lax.broadcasted_iota(jnp.int32, (slots, requests), 1)
    request_ids = jnp.where(slot_0[None, :] < -5, 0, request_ids)
    hits_0, hits_1 = slot_0[None, :] == slot_ids, slot_1[None, :] == slot_ids
    dev_of_slot = jnp.max(
        jnp.maximum(
            jnp.where(hits_0, 2 * request_ids, -1), jnp.where(hits_1, 2 * request_ids + 1, -1)
        ),
        axis=1,
    )
    new_pool = updated_pool(dev_of_slot, state_pool, returned)
    return (mixed, new_tail[None], new_pool)


def solution(mesh):
    return jax.shard_map(
        local,
        mesh=mesh,
        in_specs=(
            P("req", "ctx", None),
            P("req", "ctx", None),
            P("req", "ctx", None),
            P(),
            P(),
            P(),
            P(),
            P(),
            P(),
            P("req", None, None),
            P(("req", "ctx"), None, None),
            P(),
            P(),
            P(),
            P(),
        ),
        out_specs=(P("req", "ctx", None), P("req", None, None), P(("req", "ctx"), None, None)),
        check_vma=False,
    )
```

```python
import functools

import jax
import jax.numpy as jnp
from jax import lax
from jax.experimental import pallas as pl
from jax.experimental.pallas import tpu as pltpu
from jax.sharding import PartitionSpec as P

GROUPS = 8
LANES = 128
TAIL = 8
PARTS = 4
GRANT = 64 << 20
TOP = 88.72
F32 = jnp.float32
IN_HBM = pl.BlockSpec(memory_space=pltpu.HBM)
BF16 = jnp.bfloat16


def swapped(value):
    return lax.ppermute(value, "ctx", [(0, 1), (1, 0)])


def silu(value):
    half = 0.5 * value
    return half + half * jnp.tanh(half)


def cost(flops, nbytes, trans=0):
    return pl.CostEstimate(flops=flops, bytes_accessed=nbytes, transcendentals=trans)


def part_copies(source, target, sems, parts):
    size = source.shape[0] // parts
    return [
        pltpu.make_async_copy(
            source.at[pl.ds(c * size, size)], target.at[pl.ds(c * size, size)], sems.at[c]
        )
        for c in range(parts)
    ]


def gather_body(
    early_ref, late_ref, pool_ref, tokens_ref, out_ref, last_hbm, page_ref, round_ref, deep_ref,
    last_ref, in_sem, out_sem, deep_sem, last_sem,
):
    devices = round_ref.shape[0]
    deep = deep_ref.shape[0]
    rim = last_ref.shape[0]
    ins = part_copies(pool_ref, page_ref, in_sem, PARTS)
    outs = part_copies(round_ref, out_ref, out_sem, PARTS)
    rows = pltpu.make_async_copy(
        tokens_ref.at[0, pl.ds(tokens_ref.shape[1] - deep, deep)], deep_ref, deep_sem
    )
    rows.start()
    for copy in ins:
        copy.start()
    rows.wait()
    last_ref[...] = deep_ref[...].astype(F32)[deep - rim :].astype(BF16)
    last = pltpu.make_async_copy(last_ref, last_hbm, last_sem)
    last.start()
    for copy in ins:
        copy.wait()
    for c in range(PARTS):
        for k in range(devices // PARTS):
            device = c * (devices // PARTS) + k
            slot = (early_ref, late_ref)[device % 2][device // 2]
            round_ref[device] = page_ref[jnp.maximum(slot, 0)].astype(BF16)
        outs[c].start()
    last.wait()
    for copy in outs:
        copy.wait()


def gather_pages(slot_early, slot_late, pool, tokens, devices, rim):
    slots, rows, width = pool.shape
    channels = tokens.shape[2]
    return pl.pallas_call(
        gather_body,
        out_shape=(
            jax.ShapeDtypeStruct((devices, rows, width), BF16),
            jax.ShapeDtypeStruct((rim, channels), BF16),
        ),
        grid_spec=pltpu.PrefetchScalarGridSpec(
            num_scalar_prefetch=2,
            grid=(1,),
            in_specs=[IN_HBM, IN_HBM],
            out_specs=[IN_HBM, IN_HBM],
            scratch_shapes=[
                pltpu.VMEM((slots, rows, width), F32),
                pltpu.VMEM((devices, rows, width), BF16),
                pltpu.VMEM((16, channels), BF16),
                pltpu.VMEM((rim, channels), BF16),
                pltpu.SemaphoreType.DMA((PARTS,)),
                pltpu.SemaphoreType.DMA((PARTS,)),
                pltpu.SemaphoreType.DMA,
                pltpu.SemaphoreType.DMA,
            ],
        ),
        compiler_params=pltpu.CompilerParams(vmem_limit_bytes=GRANT),
        cost_estimate=cost(slots * rows * width, slots * rows * width * 6),
        name="gather_pages",
    )(slot_early, slot_late, pool, tokens)


def steps_body(id_ref, count_ref, raw_ref, bias_ref, alog_ref, cum_ref, shift_ref, ending_ref, decay_ref):
    rows, heads = cum_ref.shape
    pos = id_ref[1] * rows + lax.broadcasted_iota(jnp.int32, (rows, heads), 0)
    live = pos < count_ref[id_ref[0]]
    value = raw_ref[0].astype(F32) + bias_ref[...]
    soft = jnp.maximum(value, 0.0) + jnp.log1p(jnp.exp(-jnp.abs(value)))
    dt = jnp.where(live, soft, 0.0)
    la = -jnp.exp(alog_ref[...]) * dt
    tri = (
        lax.broadcasted_iota(jnp.int32, (rows, rows), 0)
        >= lax.broadcasted_iota(jnp.int32, (rows, rows), 1)
    )
    tri = jnp.where(tri, 1.0, 0.0).astype(BF16)
    high = la.astype(BF16)
    rest = la - high.astype(F32)
    mid = rest.astype(BF16)
    low = (rest - mid.astype(F32)).astype(BF16)
    cum = (
        jnp.dot(tri, low, preferred_element_type=F32)
        + jnp.dot(tri, mid, preferred_element_type=F32)
        + jnp.dot(tri, high, preferred_element_type=F32)
    )
    last = cum[rows - 1 :, :]
    cum_ref[...] = cum
    some = dt > 0.0
    log_dt = jnp.where(some, jnp.log(jnp.where(some, dt, 1.0)), -1e30)
    shift_ref[...] = (cum - log_dt).T
    ending_ref[...] = jnp.exp(last - cum) * dt
    decay_ref[...] = jnp.broadcast_to(jnp.exp(last), decay_ref.shape)


def step_tables(ids, counts, dt_raw, dt_bias, a_log):
    _, rows, heads = dt_raw.shape
    whole = lambda *shape: pl.BlockSpec(shape, lambda i, *s: (0,) * len(shape))
    return pl.pallas_call(
        steps_body,
        out_shape=(
            jax.ShapeDtypeStruct((rows, heads), F32),
            jax.ShapeDtypeStruct((heads, rows), F32),
            jax.ShapeDtypeStruct((rows, heads), F32),
            jax.ShapeDtypeStruct((8, heads), F32),
        ),
        grid_spec=pltpu.PrefetchScalarGridSpec(
            num_scalar_prefetch=2,
            grid=(1,),
            in_specs=[whole(1, rows, heads), whole(1, heads), whole(1, heads)],
            out_specs=[whole(rows, heads), whole(heads, rows), whole(rows, heads), whole(8, heads)],
        ),
        compiler_params=pltpu.CompilerParams(vmem_limit_bytes=GRANT),
        cost_estimate=cost(rows * rows * heads * 6, rows * heads * 16, rows * heads * 4),
        name="step_tables",
    )(ids, counts, dt_raw, dt_bias[None], a_log[None])


def pair_columns(table, p, first):
    rows = table.shape[0]
    left = jnp.broadcast_to(table[:, 2 * p : 2 * p + 1], (rows, LANES))
    right = jnp.broadcast_to(table[:, 2 * p + 1 : 2 * p + 2], (rows, LANES))
    return left, right, jnp.where(first, left, right)


def first_group(id_ref, own):
    ctx = id_ref[1]
    return (ctx if own else 1 - ctx) * (GROUPS // 2)


def group_heads(ref, group, per_group):
    heads = ref.shape[1]
    return pltpu.roll(ref[...], lax.rem(heads - group * per_group, heads), 1)


def conv_body(
    own, channels, id_ref, prefix_ref, count_ref, x_ref, b_ref, c_ref, cache_ref, before_ref, weight_ref, bias_ref,
    ending_ref, *rest
):
    xa_ref, bc_ref, state_ref, tail_ref, rows_ref, cols_ref = rest[-6:]
    group = first_group(id_ref, own) + pl.program_id(0)
    rows = x_ref.shape[1]
    width = x_ref.shape[2]
    nstate = b_ref.shape[2]
    pairs = width // LANES
    taps = weight_ref.shape[0]
    b_at, c_at = channels
    first = lax.broadcasted_iota(jnp.int32, (rows, LANES), 1) < LANES // 2
    cols_ref[...] = group_heads(ending_ref, group, 2 * pairs)
    held = lax.broadcasted_iota(jnp.int32, (taps - 1, LANES), 0) >= taps - 1 - prefix_ref[id_ref[0]]
    lead = id_ref[1] == 0
    last = count_ref[id_ref[0]] - id_ref[1] * rows
    newest = 9 - taps + jnp.clip(last, 0, rows)
    here = (count_ref[id_ref[0]] > rows) == (id_ref[1] == 1)
    if own:

        @pl.when(pl.program_id(0) == 0)
        def _():
            tail_ref[...] = rest[0][...]

    def conv(slot, src, at, begin):
        lanes = pl.ds(pl.multiple_of(begin, LANES), LANES)
        cached = jnp.where(held, cache_ref[0, :, lanes].astype(F32), 0.0)
        rim = jnp.where(lead, cached, before_ref[:, lanes].astype(F32))
        rows_ref[slot, 9 - taps : 8] = rim
        rows_ref[slot, 8 : 8 + rows] = src[0, :, at : at + LANES].astype(F32)
        tail_ref[:, lanes] = jnp.where(here, rows_ref[slot, pl.ds(newest, 8)], 0.0).astype(BF16)
        total = bias_ref[:, lanes]
        weight = weight_ref[:, lanes]
        for k in range(taps):
            start = 9 - taps + k
            total = total + weight[k : k + 1] * rows_ref[slot, start : start + rows]
        return silu(total).astype(BF16)

    bc_ref[:, :nstate] = conv(0, b_ref, 0, b_at + group * nstate)
    bc_ref[:, nstate:] = conv(1, c_ref, 0, c_at + group * nstate)
    b_turned = bc_ref[:, :nstate].T
    nt = (((1,), (1,)), ((), ()))
    down = lax.broadcasted_iota(jnp.int32, (LANES, LANES), 0)
    across = lax.broadcasted_iota(jnp.int32, (LANES, LANES), 1)
    same = jnp.where(down == across, 1.0, 0.0).astype(BF16)
    for p in range(pairs):
        act = conv(p % 2, x_ref, p * LANES, group * width + p * LANES)
        xa_ref[:, p * LANES : (p + 1) * LANES] = act
        _, _, ending = pair_columns(cols_ref, p, first)
        scaled = (act.astype(F32) * ending).astype(BF16)
        turned = jnp.dot(b_turned, scaled, preferred_element_type=F32).astype(BF16)
        state = lax.dot_general(same, turned, nt, preferred_element_type=F32)
        state_ref[p * LANES : (p + 1) * LANES, :] = state.astype(BF16)


def conv_half(own, ids, prefix, counts, tail, tokens, cache, before, weight, bias, ending, inner, nstate):
    _, rows, channels = tokens.shape
    heads = ending.shape[1]
    width = inner // GROUPS
    half = GROUPS // 2
    b_at, c_at = inner, inner + GROUPS * nstate

    def channel_block(wide, begin):
        return pl.BlockSpec(
            (1, rows, wide), lambda i, a, *s: (0, 0, begin // wide + first_group(a, own) + i)
        )

    def whole(value):
        return pl.BlockSpec(value.shape, lambda i, *s: (0,) * value.ndim)

    tails = [] if tail is None else [tail]
    return pl.pallas_call(
        functools.partial(conv_body, own, (b_at, c_at)),
        out_shape=(
            jax.ShapeDtypeStruct((rows, half * width), BF16),
            jax.ShapeDtypeStruct((rows, half * 2 * nstate), BF16),
            jax.ShapeDtypeStruct((half * width, nstate), BF16),
            jax.ShapeDtypeStruct((8, channels), BF16),
        ),
        grid_spec=pltpu.PrefetchScalarGridSpec(
            num_scalar_prefetch=3,
            grid=(half,),
            in_specs=[
                channel_block(width, 0),
                channel_block(nstate, b_at),
                channel_block(nstate, c_at),
                whole(cache),
                whole(before),
                whole(weight),
                whole(bias),
                whole(ending),
            ]
            + [whole(value) for value in tails],
            out_specs=[
                pl.BlockSpec((rows, width), lambda i, *s: (0, i)),
                pl.BlockSpec((rows, 2 * nstate), lambda i, *s: (0, i)),
                pl.BlockSpec((width, nstate), lambda i, *s: (i, 0)),
                pl.BlockSpec((8, channels), lambda i, *s: (0, 0)),
            ],
            scratch_shapes=[pltpu.VMEM((2, rows + 16, LANES), F32), pltpu.VMEM((rows, heads), F32)],
        ),
        compiler_params=pltpu.CompilerParams(vmem_limit_bytes=GRANT),
        cost_estimate=cost(rows * channels * 40, rows * channels * 2, rows * channels // 2),
        name="conv_half",
    )(ids, prefix, counts, tokens, tokens, tokens, cache, before, weight, bias, ending, *tails)


def owner_of(owner_ref, id_ref, page, pages):
    return owner_ref[lax.rem(id_ref[0], owner_ref.shape[0]), id_ref[1] * pages + page]


def owner_block(owners):
    deep = min(8, owners.shape[0])
    return pl.BlockSpec(
        (deep, owners.shape[1]), lambda i, d, *s: (d[0] // deep, 0), memory_space=pltpu.SMEM
    )


def decay_block(decay):
    return pl.BlockSpec(decay.shape, lambda i, *s: (0, 0), memory_space=pltpu.SMEM)


def outbound_body(id_ref, prefix_ref, owner_ref, mine_ref, theirs_ref, own_ref, recv_ref, out_ref):
    chunk, rows, width = own_ref.shape
    pages = chunk * pl.num_programs(0)
    lead = id_ref[1] == 0
    keep = jnp.where(prefix_ref[id_ref[0]] > 0, 1.0, 0.0)
    top = lax.broadcasted_iota(jnp.int32, (TAIL, width), 0) == 0
    for k in range(chunk):
        page = pl.program_id(0) * chunk + k
        head = id_ref[1] * pages + page
        mine, theirs = mine_ref[0, head], theirs_ref[0, head]
        own_w = jnp.where(lead, theirs, 1.0)
        recv_w = jnp.where(lead, 1.0, mine)
        total = own_w * own_ref[k].astype(F32) + recv_w * recv_ref[k].astype(F32)
        whole = jnp.full((TAIL, width), mine * theirs * keep, F32)
        high = whole.astype(BF16).astype(F32)
        owner = owner_of(owner_ref, id_ref, page, pages)
        out_ref[owner, :rows] = total.astype(BF16)
        out_ref[owner, rows:] = jnp.where(top, high, whole - high).astype(BF16)


def outbound_pages(ids, prefix, owners, mine, theirs, own, recv, devices):
    pages, rows, width = own.shape
    chunk = pages // 2
    return pl.pallas_call(
        outbound_body,
        out_shape=jax.ShapeDtypeStruct((devices, rows + TAIL, width), BF16),
        grid_spec=pltpu.PrefetchScalarGridSpec(
            num_scalar_prefetch=2,
            grid=(pages // chunk,),
            in_specs=[owner_block(owners), decay_block(mine), decay_block(theirs)]
            + [pl.BlockSpec((chunk, rows, width), lambda i, *s: (i, 0, 0))] * 2,
            out_specs=pl.BlockSpec((devices, rows + TAIL, width), lambda i, *s: (0, 0, 0)),
        ),
        compiler_params=pltpu.CompilerParams(vmem_limit_bytes=GRANT),
        cost_estimate=cost(pages * rows * width * 3, pages * rows * width * 8),
        name="outbound_pages",
    )(ids, prefix, owners, mine, theirs, own, recv)


def start_body(
    id_ref, prefix_ref, owner_ref, mine_ref, theirs_ref, in_ref, own_hbm, recv_hbm, start_hbm, send_hbm,
    page_ref, state_ref, held_ref, moved_ref, sem, state_sem, held_sem, moved_sem,
):
    pages = page_ref.shape[0]
    keep = jnp.where(prefix_ref[id_ref[0]] > 0, 1.0, 0.0)

    def run(decay_ref, state_hbm, held_hbm, moved_hbm):
        states = part_copies(state_hbm, state_ref, state_sem, PARTS)
        held_out = part_copies(held_ref, held_hbm, held_sem, PARTS)
        moved_out = part_copies(moved_ref, moved_hbm, moved_sem, PARTS)
        fetches = []
        for page in range(pages):
            owner = owner_of(owner_ref, id_ref, page, pages)
            fetches.append(pltpu.make_async_copy(in_ref.at[owner], page_ref.at[page], sem.at[page]))
        for c in range(PARTS):
            states[c].start()
            for k in range(pages // PARTS):
                fetches[c * (pages // PARTS) + k].start()
        for c in range(PARTS):
            states[c].wait()
            for k in range(pages // PARTS):
                fetches[c * (pages // PARTS) + k].wait()
            for k in range(pages // PARTS):
                page = c * (pages // PARTS) + k
                held = page_ref[page].astype(F32) * keep
                decay = decay_ref[0, id_ref[1] * pages + page]
                held_ref[page] = held.astype(BF16)
                moved_ref[page] = (decay * held + state_ref[page].astype(F32)).astype(BF16)
            held_out[c].start()
            moved_out[c].start()
        for copy in held_out + moved_out:
            copy.wait()

    @pl.when(id_ref[1] == 0)
    def _():
        run(mine_ref, own_hbm, start_hbm, send_hbm)

    @pl.when(id_ref[1] != 0)
    def _():
        run(theirs_ref, recv_hbm, send_hbm, start_hbm)


def start_states(ids, prefix, owners, mine, theirs, incoming, own, recv):
    pages, rows, width = own.shape
    return pl.pallas_call(
        start_body,
        out_shape=(jax.ShapeDtypeStruct(own.shape, BF16),) * 2,
        grid_spec=pltpu.PrefetchScalarGridSpec(
            num_scalar_prefetch=2,
            grid=(1,),
            in_specs=[owner_block(owners), decay_block(mine), decay_block(theirs)] + [IN_HBM] * 3,
            out_specs=[IN_HBM, IN_HBM],
            scratch_shapes=[pltpu.VMEM(own.shape, BF16)] * 4
            + [pltpu.SemaphoreType.DMA((pages,))]
            + [pltpu.SemaphoreType.DMA((PARTS,))] * 3,
        ),
        compiler_params=pltpu.CompilerParams(vmem_limit_bytes=GRANT),
        cost_estimate=cost(pages * rows * width * 4, pages * rows * width * 8),
        name="start_states",
    )(ids, prefix, owners, mine, theirs, incoming, own, recv)


def mixer_body(
    own, id_ref, count_ref, skip_ref, x_ref, bc_ref, cum_ref, shift_ref, start_ref, gate_ref,
    norm_ref, *rest
):
    out_ref, cols_ref, score_ref, gated_ref = rest[-4:]
    group = first_group(id_ref, own) + pl.program_id(0)
    rows, width = x_ref.shape
    pairs = width // LANES
    half = rows // 2
    first = lax.broadcasted_iota(jnp.int32, (rows, LANES), 1) < LANES // 2
    cols_ref[...] = group_heads(cum_ref, group, 2 * pairs)
    nstate = start_ref.shape[1]
    b_val, c_val = bc_ref[:, :nstate], bc_ref[:, nstate:]
    nt = (((1,), (1,)), ((), ()))
    scores = lax.dot_general(c_val, b_val, nt, preferred_element_type=F32)
    lower = (
        lax.broadcasted_iota(jnp.int32, (rows, rows), 0)
        >= lax.broadcasted_iota(jnp.int32, (rows, rows), 1)
    )
    score_ref[...] = jnp.where(lower, scores, 0.0)
    squares = jnp.zeros((rows, LANES), F32)
    for p in range(pairs):
        lanes = slice(p * LANES, (p + 1) * LANES)
        x_val = x_ref[:, lanes]
        left, right, both = pair_columns(cols_ref, p, first)
        ys = []
        for cum, h in ((left, 2 * p), (right, 2 * p + 1)):
            early = shift_ref[h : h + 1, :half]
            late = shift_ref[h : h + 1, half:]
            w00 = score_ref[:half, :half] * jnp.exp(jnp.minimum(cum[:half] - early, TOP))
            w10 = score_ref[half:, :half] * jnp.exp(cum[half:] - early)
            w11 = score_ref[half:, half:] * jnp.exp(jnp.minimum(cum[half:] - late, TOP))
            y0 = jnp.dot(w00.astype(BF16), x_val[:half], preferred_element_type=F32)
            w1 = jnp.concatenate([w10.astype(BF16), w11.astype(BF16)], axis=1)
            y1 = jnp.dot(w1, x_val, preferred_element_type=F32)
            ys.append(jnp.concatenate([y0, y1], axis=0))
        carried = lax.dot_general(c_val, start_ref[lanes, :], nt, preferred_element_type=F32)
        y = jnp.where(first, ys[0], ys[1]) + jnp.exp(both) * carried
        head = group * 2 * pairs + 2 * p
        skip = jnp.where(first, skip_ref[head], skip_ref[head + 1])
        y = y + skip * x_val.astype(F32)
        gated = y * silu(gate_ref[0, :, lanes].astype(F32))
        gated_ref[p] = gated
        squares = squares + gated * gated
    mean = jnp.sum(squares, axis=1, keepdims=True) * (1.0 / width)
    pos = id_ref[1] * rows + lax.broadcasted_iota(jnp.int32, (rows, 1), 0)
    live = pos < count_ref[id_ref[0]]
    factor = jnp.where(live, lax.rsqrt(mean + 1e-05), 0.0)
    factor = jnp.broadcast_to(factor, (rows, LANES))
    for p in range(pairs):
        lanes = slice(p * LANES, (p + 1) * LANES)
        at = pl.ds(pl.multiple_of(group * width + p * LANES, LANES), LANES)
        out_ref[0, :, lanes] = (gated_ref[p] * factor * norm_ref[:, at]).astype(BF16)


def mixer_half(own, ids, counts, skip, x, bc, cum, shift, start, gate, norm, so_far):
    rows, half_width = x.shape
    heads = cum.shape[1]
    half = GROUPS // 2
    width = half_width // half
    nstate = start.shape[1]
    per_group = heads // GROUPS
    in_specs = [
        pl.BlockSpec((rows, width), lambda i, a, *s: (0, i)),
        pl.BlockSpec((rows, 2 * nstate), lambda i, a, *s: (0, i)),
        pl.BlockSpec((rows, heads), lambda i, a, *s: (0, 0)),
        pl.BlockSpec((per_group, rows), lambda i, a, *s: (first_group(a, own) + i, 0)),
        pl.BlockSpec((width, nstate), lambda i, a, *s: (i, 0)),
        pl.BlockSpec((1, rows, width), lambda i, a, *s: (0, 0, first_group(a, own) + i)),
        pl.BlockSpec(norm.shape, lambda i, a, *s: (0, 0)),
    ]
    args = [ids, counts, skip, x, bc, cum, shift, start, gate, norm]
    aliases = {}
    if so_far is not None:
        in_specs.append(pl.BlockSpec(memory_space=pl.ANY))
        aliases = {len(args): 0}
        args.append(so_far)
    return pl.pallas_call(
        functools.partial(mixer_body, own),
        out_shape=jax.ShapeDtypeStruct(gate.shape, BF16),
        grid_spec=pltpu.PrefetchScalarGridSpec(
            num_scalar_prefetch=3,
            grid=(half,),
            in_specs=in_specs,
            out_specs=pl.BlockSpec((1, rows, width), lambda i, a, *s: (0, 0, first_group(a, own) + i)),
            scratch_shapes=[
                pltpu.VMEM((rows, heads), F32),
                pltpu.VMEM((rows, rows), F32),
                pltpu.VMEM((width // LANES, rows, LANES), F32),
            ],
        ),
        input_output_aliases=aliases,
        compiler_params=pltpu.CompilerParams(vmem_limit_bytes=GRANT),
        cost_estimate=cost(
            rows * half_width * (2 * rows + 2 * nstate), rows * half_width * 8, rows * rows * heads // 2
        ),
        name="mixer_half",
    )(*args)


def pool_body(dev_ref, pool_hbm, in_hbm, out_hbm, in_ref, pool_ref, new_ref, in_sem, pool_sem, out_sem):
    slots, rows, _ = pool_ref.shape
    parts = 2 * PARTS
    size = slots // parts
    pages = part_copies(in_hbm, in_ref, in_sem, PARTS)
    pools = part_copies(pool_hbm, pool_ref, pool_sem, parts)
    outs = part_copies(new_ref, out_hbm, out_sem, parts)
    for copy in pages + pools:
        copy.start()
    for copy in pages:
        copy.wait()
    for c in range(parts):
        pools[c].wait()
        for k in range(size):
            slot = c * size + k
            device = dev_ref[slot]
            at = jnp.maximum(device, 0)
            tail = in_ref[at, rows:].astype(F32)
            whole = tail[0:1] + tail[1:2]
            old = pool_ref[slot]
            new = whole * old + in_ref[at, :rows].astype(F32)
            new_ref[slot] = jnp.where(device >= 0, new, old)
        outs[c].start()
    for copy in outs:
        copy.wait()


def updated_pool(dev_of_slot, pool, returned):
    slots, rows, width = pool.shape
    return pl.pallas_call(
        pool_body,
        out_shape=jax.ShapeDtypeStruct(pool.shape, F32),
        grid_spec=pltpu.PrefetchScalarGridSpec(
            num_scalar_prefetch=1,
            grid=(1,),
            in_specs=[IN_HBM, IN_HBM],
            out_specs=IN_HBM,
            scratch_shapes=[
                pltpu.VMEM(returned.shape, BF16),
                pltpu.VMEM(pool.shape, F32),
                pltpu.VMEM(pool.shape, F32),
                pltpu.SemaphoreType.DMA((PARTS,)),
                pltpu.SemaphoreType.DMA((2 * PARTS,)),
                pltpu.SemaphoreType.DMA((2 * PARTS,)),
            ],
        ),
        compiler_params=pltpu.CompilerParams(vmem_limit_bytes=GRANT),
        cost_estimate=cost(slots * rows * width * 2, slots * rows * width * 10),
        name="updated_pool",
    )(dev_of_slot, pool, returned)


def local(
    conv_input,
    gate_input,
    dt_raw,
    conv_weight,
    conv_bias,
    dt_bias,
    a_log,
    d_skip,
    norm_weight,
    conv_cache,
    state_pool,
    page_owner,
    page_slot,
    prefix_len,
    new_count,
):
    ctx_count = lax.axis_size("ctx")
    devices = lax.axis_size("req") * ctx_count
    req_index = lax.axis_index("req")
    ctx_index = lax.axis_index("ctx")
    own_index = req_index * ctx_count + ctx_index
    rows = conv_input.shape[1]
    heads = dt_raw.shape[2]
    inner = gate_input.shape[2]
    slots, page_rows, nstate = state_pool.shape
    pages = page_owner.shape[1] // ctx_count
    rim = conv_weight.shape[0] - 1
    requests = page_owner.shape[0]

    matches = page_owner == own_index
    early = jnp.arange(2 * pages)[None, :] < pages
    slot_0 = jnp.max(jnp.where(matches & early, page_slot, -1), axis=1)
    slot_1 = jnp.max(jnp.where(matches & ~early, page_slot, -1), axis=1)
    outgoing, last_rows = gather_pages(slot_0, slot_1, state_pool, conv_input, devices, rim)
    outgoing, conv_input, dt_raw, new_count, prefix_len, page_owner = lax.optimization_barrier(
        (outgoing, conv_input, dt_raw, new_count, prefix_len, page_owner)
    )
    incoming = lax.all_to_all(outgoing, ("req", "ctx"), split_axis=0, concat_axis=0, tiled=True)

    ids = jnp.stack([req_index, ctx_index]).astype(jnp.int32)
    previous = lax.ppermute(last_rows, "ctx", [(0, 1)])
    cum, shift, ending, decay_rows = step_tables(ids, new_count, dt_raw, dt_bias, a_log)
    other_decay = swapped(decay_rows)

    conv_args = (
        conv_input, conv_cache, previous, conv_weight, conv_bias[None], ending, inner, nstate
    )
    x_other, bc_other, state_other, tail = conv_half(False, ids, prefix_len, new_count, None, *conv_args)
    received = swapped(state_other)
    x_own, bc_own, state_own, tail = conv_half(True, ids, prefix_len, new_count, tail, *conv_args)
    as_pages = lambda value: value.reshape(pages, page_rows, nstate)
    own_pages, recv_pages = as_pages(state_own), as_pages(received)
    page_args = (ids, prefix_len, page_owner, decay_rows, other_decay)
    outbound = outbound_pages(*page_args, own_pages, recv_pages, devices)
    returned = lax.all_to_all(outbound, ("req", "ctx"), split_axis=0, concat_axis=0, tiled=True)

    start, send = start_states(*page_args, incoming, own_pages, recv_pages)
    start, slot_0, slot_1, tail = lax.optimization_barrier(
        (start, slot_0, slot_1, tail)
    )
    start_other = swapped(send)
    as_rows = lambda value: value.reshape(pages * page_rows, nstate)
    mixed = mixer_half(
        True, ids, new_count, d_skip, x_own, bc_own, cum, shift, as_rows(start), gate_input,
        norm_weight[None], None,
    )
    mixed = mixer_half(
        False, ids, new_count, d_skip, x_other, bc_other, cum, shift, as_rows(start_other),
        gate_input, norm_weight[None], mixed,
    )

    new_tail = (tail + swapped(tail))[:rim]
    slot_ids = lax.broadcasted_iota(jnp.int32, (slots, requests), 0)
    request_ids = lax.broadcasted_iota(jnp.int32, (slots, requests), 1)
    request_ids = jnp.where(slot_0[None, :] < -5, 0, request_ids)
    hits_0, hits_1 = slot_0[None, :] == slot_ids, slot_1[None, :] == slot_ids
    dev_of_slot = jnp.max(
        jnp.maximum(
            jnp.where(hits_0, 2 * request_ids, -1), jnp.where(hits_1, 2 * request_ids + 1, -1)
        ),
        axis=1,
    )
    new_pool = updated_pool(dev_of_slot, state_pool, returned)
    return (mixed, new_tail[None], new_pool)


def solution(mesh):
    return jax.shard_map(
        local,
        mesh=mesh,
        in_specs=(
            P("req", "ctx", None),
            P("req", "ctx", None),
            P("req", "ctx", None),
            P(),
            P(),
            P(),
            P(),
            P(),
            P(),
            P("req", None, None),
            P(("req", "ctx"), None, None),
            P(),
            P(),
            P(),
            P(),
        ),
        out_specs=(P("req", "ctx", None), P("req", None, None), P(("req", "ctx"), None, None)),
        check_vma=False,
    )
```
